128 devices in a mesh: section: 8 (over y, core), tensor: 16 (over z, x).
Axes of the slice: x: 4, y: 4, z: 4, core: 2. Of those that a mesh axis runs over, the one named last changes fastest.
Arguments:
- resid: bfloat16 [64, 4608], P('section', 'tensor'), may hold values from -6 to 6
- pre_gain: float32 [8, 4608], P('section'), may hold values from 0.5 to 1.5
- post_gain: float32 [8, 4608], P('section'), may hold values from 0.5 to 1.5
- w_query: bfloat16 [8, 4608, 4096], P('section', None, 'tensor'), may hold values from -0.09375 to 0.09375
- w_key: bfloat16 [8, 4608, 2048], P('section', None, 'tensor'), may hold values from -0.09375 to 0.09375
- w_value: bfloat16 [8, 4608, 2048], P('section', None, 'tensor'), may hold values from -0.09375 to 0.09375
- w_out: bfloat16 [8, 4096, 4608], P('section', 'tensor'), may hold values from -0.09375 to 0.09375
- key_cache: bfloat16 [8, 64, 16, 64, 128], P('section', None, 'tensor'), may hold values from -6 to 6
- value_cache: bfloat16 [8, 64, 16, 64, 128], P('section', None, 'tensor'), may hold values from -6 to 6
- lengths: int32 [64], replicated, may hold values from 1 to 64, as said below
- concept: int32 [64], replicated, may hold values from 0 to 511
- steer_layer: int32 [64], replicated, may hold values from 0 to 7
- strength: float32 [64], replicated, may hold values from 0.5 to 2
- directions: bfloat16 [512, 4608], P(None, 'tensor'), may hold values from -6 to 6
Outputs:
- final_resid: bfloat16 [64, 4608], P('section', 'tensor')
The draws below stay inside these ranges and needn't reach their ends.
Inputs may be any that keep to these rules, and one draw needn't show every extreme that they name: `lengths`: some row of every draw has exactly 64.
All inputs are finite; a program needn't handle non-finite values.
Results may differ from the reference program's by a relative error of at most 0.03.
Values may be sent and summed in bfloat16 or wider, within the bound.
No kernel may reach another device: no remote copies, remote signals or barrier semaphores. Data moves between devices by JAX's collectives and lax.ppermute only.
A program may use at most 64 MiB of HBM per device.

```python
import math
import jax
import jax.numpy as jnp
import numpy as np
from jax import lax

D = 4608
HEADS = 32
KVH = 16
HD = 128
CONCEPTS = 512
CTX = 64
ROWS = 64
LAYERS = 8


def draw_lengths(key, part):
    values = jax.random.randint(key, (ROWS,), 1, CTX + 1, dtype=jnp.int32)
    return values.at[0].set(CTX)


def touch_ends(result, stream_key, low, high):
    spot = [jax.random.randint(jax.random.fold_in(stream_key, axis), (), 0, length) for axis, length in enumerate(result.shape)]
    widest = result.shape.index(max(result.shape))
    neighbour = spot[:widest] + [(spot[widest] + 1) % result.shape[widest]] + spot[widest + 1:]
    return result.at[tuple(spot)].set(low).at[tuple(neighbour)].set(high)


def levels(own_key, dims, cuts, smallest, high):
    loudness = 1.0
    for dim, shards_of in cuts:
        heights = jax.random.uniform(jax.random.fold_in(jax.random.fold_in(own_key, 6), dim), (shards_of,), jnp.float32, smallest / len(cuts), high / len(cuts))
        loudness = loudness * jnp.repeat(jnp.exp(heights), dims[dim] // shards_of).reshape((-1,) + (1,) * (len(dims) - 1 - dim))
    return loudness


def rank_table(amount, slope):
    portions = [(1 << 20) // math.isqrt(rank ** slope) + 1 for rank in range(1, amount + 1)]
    deviation = 1 + sum(portions) // (1 << 30)
    return np.cumsum(np.array([max(1, weight // deviation) for weight in portions]))


def skewed_ids(stream_key, shape, count, lean):
    grid = rank_table(count, lean)
    lot = jax.random.randint(jax.random.fold_in(stream_key, 1), shape, 0, int(grid[count - 1]))
    standing = jnp.searchsorted(jnp.asarray(grid, jnp.int32), lot, side="right")
    return jax.random.permutation(jax.random.fold_in(stream_key, 2), count)[standing].astype(jnp.int32)


def scatter_about(rng, shape, scale, bound, pieces=(), kind=jnp.bfloat16):
    entries = scale * jax.random.normal(rng, shape, jnp.float32)
    if pieces:
        entries = entries * levels(rng, shape, pieces, -0.22, 0.18)
    return jnp.clip(entries, -bound, bound).astype(kind)


def setup_inputs(seed: int = 0) -> dict:
    streams_of = jax.random.split(jax.random.key(seed), 15)
    return {
        "resid": scatter_about(streams_of[0], (ROWS, D), 1.0, 6.0, ((0, 8), (1, 16))),
        "pre_gain": jnp.clip(1.0 + 0.1 * jax.random.normal(streams_of[1], (LAYERS, D), jnp.float32), 0.5, 1.5),
        "post_gain": jnp.clip(1.0 + 0.1 * jax.random.normal(streams_of[2], (LAYERS, D), jnp.float32), 0.5, 1.5),
        "w_query": scatter_about(streams_of[3], (LAYERS, D, HEADS * HD), D ** -0.5, 0.09375, ((0, 8), (2, 16))),
        "w_key": scatter_about(streams_of[4], (LAYERS, D, KVH * HD), D ** -0.5, 0.09375, ((0, 8), (2, 16))),
        "w_value": scatter_about(streams_of[5], (LAYERS, D, KVH * HD), D ** -0.5, 0.09375, ((0, 8), (2, 16))),
        "w_out": scatter_about(streams_of[6], (LAYERS, HEADS * HD, D), (HEADS * HD) ** -0.5, 0.09375, ((0, 8), (1, 16))),
        "key_cache": scatter_about(streams_of[7], (LAYERS, ROWS, KVH, CTX, HD), 1.0, 6.0, ((0, 8), (2, 16))),
        "value_cache": scatter_about(streams_of[8], (LAYERS, ROWS, KVH, CTX, HD), 1.0, 6.0, ((0, 8), (2, 16))),
        "lengths": draw_lengths(jax.random.fold_in(streams_of[14], 71), 0),
        "concept": touch_ends(skewed_ids(streams_of[10], (ROWS,), CONCEPTS, 2), jax.random.fold_in(streams_of[10], 3), 0, CONCEPTS - 1).astype(jnp.int32),
        "steer_layer": touch_ends(jax.random.randint(streams_of[11], (ROWS,), 0, LAYERS), jax.random.fold_in(streams_of[11], 1), 0, LAYERS - 1).astype(jnp.int32),
        "strength": jnp.clip(jax.random.uniform(streams_of[12], (ROWS,), jnp.float32, 0.5, 2.0), 0.5, 2.0),
        "directions": scatter_about(streams_of[13], (CONCEPTS, D), 1.0, 6.0, ((1, 16),)),
    }


epsilon = 1e-06
softcap_limit = 50.0

def rotate(vectors, places):
    half_dim = vectors.shape[-1] // 2
    frequency = 10000.0 ** (-(jnp.arange(half_dim, dtype=jnp.float32) * 2.0) / vectors.shape[-1])
    angles = places[:, None, None] * frequency[None, None, :]
    first = vectors[..., :half_dim]
    second = vectors[..., half_dim:]
    cosine = jnp.cos(angles)
    sine = jnp.sin(angles)
    return jnp.concatenate([first * cosine - second * sine, second * cosine + first * sine], axis=-1)

def attend(queries, new_keys, new_values, cache_keys, cache_values, row_lengths, scale):
    scores = jnp.einsum('rkgd,rkcd->rkgc', queries.astype(jnp.float32), cache_keys.astype(jnp.float32)) * scale
    own_score = jnp.einsum('rkgd,rkd->rkg', queries.astype(jnp.float32), new_keys.astype(jnp.float32)) * scale
    capped = softcap_limit * jnp.tanh(scores / softcap_limit)
    own_capped = softcap_limit * jnp.tanh(own_score / softcap_limit)
    valid = jnp.arange(cache_keys.shape[2], dtype=jnp.int32)[None, :] < row_lengths[:, None]
    weights = jnp.where(valid[:, None, None, :], jnp.exp(capped - softcap_limit), jnp.float32(0.0))
    own_weight = jnp.exp(own_capped - softcap_limit)
    totals = lax.optimization_barrier(jnp.sum(weights, axis=-1)) + own_weight
    probs = (weights / totals[..., None]).astype(jnp.bfloat16)
    own_prob = (own_weight / totals).astype(jnp.bfloat16)
    mixed = jnp.einsum('rkgc,rkcd->rkgd', probs.astype(jnp.float32), cache_values.astype(jnp.float32))
    return mixed + own_prob.astype(jnp.float32)[..., None] * new_values.astype(jnp.float32)[:, :, None, :]

def reference(resid, pre_gain, post_gain, w_query, w_key, w_value, w_out, key_cache, value_cache, lengths, concept, steer_layer, strength, directions):
    group = HEADS // KVH
    scale = float(D // HEADS) ** (-0.5)
    places = lengths.astype(jnp.float32)
    steer_vectors = directions[concept].astype(jnp.float32)
    current = resid
    for layer_index in range(LAYERS):
        values_full = current.astype(jnp.float32)
        normed = (values_full * lax.rsqrt(lax.optimization_barrier(jnp.mean(values_full * values_full, axis=-1, keepdims=True)) + epsilon) * pre_gain[layer_index]).astype(jnp.bfloat16)
        queries = rotate(jnp.dot(normed, w_query[layer_index], preferred_element_type=jnp.float32).reshape(ROWS, HEADS, HD), places).astype(jnp.bfloat16)
        new_keys = rotate(jnp.dot(normed, w_key[layer_index], preferred_element_type=jnp.float32).reshape(ROWS, KVH, HD), places).astype(jnp.bfloat16)
        new_values = jnp.dot(normed, w_value[layer_index], preferred_element_type=jnp.float32).astype(jnp.bfloat16).reshape(ROWS, KVH, HD)
        mixed = attend(queries.reshape(ROWS, KVH, group, HD), new_keys, new_values, key_cache[layer_index], value_cache[layer_index], lengths, scale)
        heads_out = mixed.reshape(ROWS, HEADS * HD).astype(jnp.bfloat16)
        summed = jnp.dot(heads_out, w_out[layer_index], preferred_element_type=jnp.float32)
        post = summed * lax.rsqrt(lax.optimization_barrier(jnp.mean(summed * summed, axis=-1, keepdims=True)) + epsilon) * post_gain[layer_index]
        steer_gate = strength * (steer_layer == layer_index).astype(jnp.float32)
        current = (values_full + post + steer_gate[:, None] * steer_vectors).astype(jnp.bfloat16)
    return current
```

```python
import jax
import jax.numpy as jnp
from jax import lax
from jax.experimental import pallas as pl
from jax.experimental.pallas import tpu as pltpu
from jax.sharding import PartitionSpec as P

D = 4608
HEADS = 32
KVH = 16
HD = 128
GROUP = HEADS // KVH
QW = GROUP * HD
CHUNKS = 6
DC = D // CHUNKS
EPS = 1e-06
CAP = 50.0
SCALE = float(D // HEADS) ** (-0.5)
VMEM = pl.BlockSpec(memory_space=pltpu.VMEM)
ANY = pl.BlockSpec(memory_space=pl.ANY)


def turn(v, cos, sin):
    return v * cos + pltpu.roll(v, HD // 2, 1) * sin


def layer_kernel(
    x_ref, pre_ref, cos_ref, sin_ref, len_ref,
    wq_hbm, wk_hbm, wv_hbm, wo_hbm, kc_hbm, vc_hbm,
    o_ref,
    xs, w, wo, kc, vc, ho, wsem, sem,
):
    rows = xs.shape[0]
    ctx = kc.shape[1]
    blocks, per = x_ref.shape[0], x_ref.shape[1]
    copies = []
    for c in range(CHUNKS):
        at = pl.ds(c * DC, DC)
        copies.append([
            pltpu.make_async_copy(wq_hbm.at[at], w.at[at, pl.ds(0, QW)], wsem.at[3 * c]),
            pltpu.make_async_copy(wk_hbm.at[at], w.at[at, pl.ds(QW, HD)], wsem.at[3 * c + 1]),
            pltpu.make_async_copy(wv_hbm.at[at], w.at[at, pl.ds(QW + HD, HD)], wsem.at[3 * c + 2]),
        ])
    kcopy = pltpu.make_async_copy(kc_hbm, kc, sem.at[0])
    vcopy = pltpu.make_async_copy(vc_hbm, vc, sem.at[1])
    ocopy = pltpu.make_async_copy(wo_hbm, wo, sem.at[2])
    for group in copies:
        for copy in group:
            copy.start()
    kcopy.start()
    vcopy.start()
    ocopy.start()

    for b in range(blocks):
        xs[pl.ds(b * per, per), :] = x_ref[b]
    acc = jnp.zeros((rows, QW + 2 * HD), jnp.float32)
    squares = jnp.zeros((rows, 1), jnp.float32)
    for c in range(CHUNKS):
        part = xs[:, pl.ds(c * DC, DC)].astype(jnp.float32)
        squares += jnp.sum(part * part, axis=1, keepdims=True)
        scaled = (part * pre_ref[:, pl.ds(c * DC, DC)]).astype(jnp.bfloat16)
        for copy in copies[c]:
            copy.wait()
        acc += jnp.dot(scaled, w[pl.ds(c * DC, DC), :], preferred_element_type=jnp.float32)
    acc = acc * lax.rsqrt(squares / D + EPS)
    cos, sin = cos_ref[...], sin_ref[...]
    heads = [turn(acc[:, h * HD:(h + 1) * HD], cos, sin).astype(jnp.bfloat16) for h in range(GROUP)]
    new_k = turn(acc[:, QW:QW + HD], cos, sin).astype(jnp.bfloat16).astype(jnp.float32)
    new_v = acc[:, QW + HD:].astype(jnp.bfloat16).astype(jnp.float32)
    kcopy.wait()
    vcopy.wait()
    n = 8
    col = lax.broadcasted_iota(jnp.int32, (GROUP * n, n * ctx), 1)
    row = lax.broadcasted_iota(jnp.int32, (GROUP * n, n * ctx), 0)
    rel = col - (row % n) * ctx
    for g in range(rows // n):
        lo, hi = g * n, (g + 1) * n
        q = jnp.concatenate([h[lo:hi].astype(jnp.float32) for h in heads], axis=0)
        nk = jnp.concatenate([new_k[lo:hi]] * GROUP, axis=0)
        nv = jnp.concatenate([new_v[lo:hi]] * GROUP, axis=0)
        ln = jnp.concatenate([len_ref[lo:hi, :]] * GROUP, axis=0)
        keys = kc[pl.ds(lo, n)].reshape(n * ctx, HD)
        vals = vc[pl.ds(lo, n)].reshape(n * ctx, HD)
        s = lax.dot_general(
            q.astype(jnp.bfloat16), keys, (((1,), (1,)), ((), ())), preferred_element_type=jnp.float32
        )
        own = jnp.sum(q * nk, axis=1, keepdims=True)
        wt = jnp.exp(CAP * jnp.tanh(s * (SCALE / CAP)) - CAP)
        wt = jnp.where((rel >= 0) & (rel < ln), wt, 0.0)
        own_w = jnp.exp(CAP * jnp.tanh(own * (SCALE / CAP)) - CAP)
        total = jnp.sum(wt, axis=1, keepdims=True) + own_w
        probs = (wt / total).astype(jnp.bfloat16)
        own_p = (own_w / total).astype(jnp.bfloat16).astype(jnp.float32)
        mixed = jnp.dot(probs, vals, preferred_element_type=jnp.float32) + own_p * nv
        for h in range(GROUP):
            ho[pl.ds(lo, n), pl.ds(h * HD, HD)] = mixed[h * n:(h + 1) * n]
    ocopy.wait()
    lhs = ho[...].astype(jnp.bfloat16)
    for c in range(CHUNKS):
        at = pl.ds(c * DC, DC)
        out = jnp.dot(lhs, wo[:, at], preferred_element_type=jnp.float32).astype(jnp.bfloat16)
        for b in range(blocks):
            o_ref[b, :, at] = out[b * per:(b + 1) * per]


def layer_call(x, pre, cos, sin, lens, wq, wk, wv, wo, kc, vc):
    rows = kc.shape[0]
    return pl.pallas_call(
        layer_kernel,
        out_shape=jax.ShapeDtypeStruct(x.shape, jnp.bfloat16),
        in_specs=[VMEM] * 5 + [ANY] * 6,
        out_specs=VMEM,
        scratch_shapes=[
            pltpu.VMEM((rows, D), jnp.bfloat16),
            pltpu.VMEM((D, QW + 2 * HD), jnp.bfloat16),
            pltpu.VMEM(wo.shape, jnp.bfloat16),
            pltpu.VMEM(kc.shape, jnp.bfloat16),
            pltpu.VMEM(vc.shape, jnp.bfloat16),
            pltpu.VMEM((rows, QW), jnp.float32),
            pltpu.SemaphoreType.DMA((3 * CHUNKS,)),
            pltpu.SemaphoreType.DMA((3,)),
        ],
        compiler_params=pltpu.CompilerParams(vmem_limit_bytes=32 << 20),
        name="layer",
    )(x, pre, cos, sin, lens, wq, wk, wv, wo, kc, vc)


def combine_kernel(p_ref, x_ref, post_ref, steer_ref, o_ref):
    total = p_ref[0].astype(jnp.float32)
    for b in range(1, p_ref.shape[0]):
        total += p_ref[b].astype(jnp.float32)
    factor = lax.rsqrt(jnp.mean(total * total, axis=1, keepdims=True) + EPS)
    post = total * factor * post_ref[...]
    o_ref[...] = (x_ref[...].astype(jnp.float32) + post + steer_ref[...]).astype(jnp.bfloat16)


def combine_call(parts, x, post, steer):
    return pl.pallas_call(
        combine_kernel,
        out_shape=jax.ShapeDtypeStruct(x.shape, jnp.bfloat16),
        in_specs=[VMEM] * 4,
        out_specs=VMEM,
        compiler_params=pltpu.CompilerParams(vmem_limit_bytes=8 << 20),
        name="combine",
    )(parts, x, post, steer)


def swap(value, axis):
    return lax.all_to_all(value, axis, 0, 0, tiled=True)


def on_device(
    resid, pre_gain, post_gain, w_query, w_key, w_value, w_out, key_cache, value_cache,
    lengths, concept, steer_layer, strength, directions,
):
    sections = lax.axis_size("section")
    lanes = lax.axis_size("tensor")
    section = lax.axis_index("section")
    lane = lax.axis_index("tensor")
    batch, width = resid.shape
    rows = batch * sections
    per = rows // lanes

    half = HD // 2
    frequency = 10000.0 ** (-(jnp.arange(half, dtype=jnp.float32) * 2.0) / HD)
    angles = lengths.astype(jnp.float32)[:, None] * frequency[None, :]
    cosine, sine = jnp.cos(angles), jnp.sin(angles)
    cos = jnp.concatenate([cosine, cosine], axis=1)
    sin = jnp.concatenate([-sine, sine], axis=1)
    lens = lengths[:, None]

    everyone = swap(jnp.broadcast_to(resid[None], (sections, batch, width)), "section")
    one_hot = (concept[:, None] == jnp.arange(directions.shape[0], dtype=jnp.int32)[None, :])
    picked = jnp.dot(one_hot.astype(jnp.bfloat16), directions, preferred_element_type=jnp.float32)
    both = jnp.concatenate(
        [everyone.reshape(lanes, per, 1, width), picked.astype(jnp.bfloat16).reshape(lanes, per, 1, width)],
        axis=2,
    )
    both = swap(both, "tensor").transpose(2, 1, 0, 3).reshape(2, per, D)
    gate = strength * (steer_layer == section).astype(jnp.float32)
    gate = lax.dynamic_slice_in_dim(gate, lane * per, per, 0)
    steer = gate[:, None] * both[1].astype(jnp.float32)
    weights = (w_query[0], w_key[0], w_value[0], w_out[0],
               key_cache.reshape(rows, *key_cache.shape[3:]), value_cache.reshape(rows, *value_cache.shape[3:]))
    onward = [(s * lanes + t, ((s + 1) % sections) * lanes + t) for s in range(sections) for t in range(lanes)]

    def layer(x):
        full = swap(jnp.broadcast_to(x[None], (lanes, per, D)), "tensor")
        parts = layer_call(full, pre_gain, cos, sin, lens, *weights)
        parts = swap(parts, "tensor")
        return combine_call(parts, x, post_gain, steer)

    def step(s, x):
        x = lax.cond(section == s, layer, lambda v: v, x)
        return lax.ppermute(x, ("section", "tensor"), onward)

    x = lax.fori_loop(0, sections, step, both[0])
    pieces = swap(x.reshape(per, lanes, width).transpose(1, 0, 2), "tensor")
    return swap(pieces.reshape(sections, batch, width), "section")[0]


def solution(mesh):
    placed = (
        P("section", "tensor"),
        P("section", None),
        P("section", None),
        P("section", None, "tensor"),
        P("section", None, "tensor"),
        P("section", None, "tensor"),
        P("section", "tensor", None),
        P("section", None, "tensor", None, None),
        P("section", None, "tensor", None, None),
        P(),
        P(),
        P(),
        P(),
        P(None, "tensor"),
    )
    return jax.shard_map(
        on_device, mesh=mesh, in_specs=placed, out_specs=P("section", "tensor"), check_vma=False
    )
```

```python
import jax
import jax.numpy as jnp
from jax import lax
from jax.experimental import pallas as pl
from jax.experimental.pallas import tpu as pltpu
from jax.sharding import PartitionSpec as P

D = 4608
HEADS = 32
KVH = 16
HD = 128
GROUP = HEADS // KVH
QW = GROUP * HD
CHUNKS = 6
DC = D // CHUNKS
EPS = 1e-06
CAP = 50.0
SCALE = float(D // HEADS) ** (-0.5)
VMEM = pl.BlockSpec(memory_space=pltpu.VMEM)
ANY = pl.BlockSpec(memory_space=pl.ANY)


def turn(v, cos, sin):
    return v * cos + pltpu.roll(v, HD // 2, 1) * sin


def layer_kernel(
    sel_ref, x_ref, pre_ref, cos_ref, sin_ref, len_ref,
    wq_a, wk_a, wv_a, wo_a, kc_a, vc_a,
    wq_b, wk_b, wv_b, wo_b, kc_b, vc_b,
    o_ref,
    xs, w, wo, kc, vc, ho, wsem, sem,
):
    rows = xs.shape[0]
    ctx = kc.shape[1]
    blocks, per = o_ref.shape[0], o_ref.shape[1]
    mine = pl.ds(pl.multiple_of(sel_ref[1] * rows, rows), rows)

    def copies(wq_hbm, wk_hbm, wv_hbm, wo_hbm, kc_hbm, vc_hbm):
        steps = []
        for c in range(CHUNKS):
            at = pl.ds(c * DC, DC)
            steps.append([
                pltpu.make_async_copy(wq_hbm.at[at], w.at[at, pl.ds(0, QW)], wsem.at[3 * c]),
                pltpu.make_async_copy(wk_hbm.at[at], w.at[at, pl.ds(QW, HD)], wsem.at[3 * c + 1]),
                pltpu.make_async_copy(wv_hbm.at[at], w.at[at, pl.ds(QW + HD, HD)], wsem.at[3 * c + 2]),
            ])
        steps.append([
            pltpu.make_async_copy(kc_hbm.at[mine], kc, sem.at[0]),
            pltpu.make_async_copy(vc_hbm.at[mine], vc, sem.at[1]),
        ])
        steps.append([pltpu.make_async_copy(wo_hbm, wo, sem.at[2])])
        return steps

    def begin(steps):
        for step in steps:
            for copy in step:
                copy.start()

    first = copies(wq_a, wk_a, wv_a, wo_a, kc_a, vc_a)

    @pl.when(sel_ref[0] == 0)
    def _():
        begin(first)

    @pl.when(sel_ref[0] != 0)
    def _():
        begin(copies(wq_b, wk_b, wv_b, wo_b, kc_b, vc_b))

    def arrived(step):
        for copy in first[step]:
            copy.wait()

    if x_ref.shape[1] == per:
        for b in range(blocks):
            xs[pl.ds(b * per, per), :] = x_ref[b]
    else:
        width = x_ref.shape[2]
        for b in range(blocks):
            xs[:, pl.ds(b * width, width)] = x_ref[b, pl.ds(0, rows), :]
    acc = jnp.zeros((rows, QW + 2 * HD), jnp.float32)
    squares = jnp.zeros((rows, 1), jnp.float32)
    for c in range(CHUNKS):
        part = xs[:, pl.ds(c * DC, DC)].astype(jnp.float32)
        squares += jnp.sum(part * part, axis=1, keepdims=True)
        scaled = (part * pre_ref[:, pl.ds(c * DC, DC)]).astype(jnp.bfloat16)
        arrived(c)
        acc += jnp.dot(scaled, w[pl.ds(c * DC, DC), :], preferred_element_type=jnp.float32)
    acc = acc * lax.rsqrt(squares / D + EPS)
    cos, sin = cos_ref[...], sin_ref[...]
    heads = [turn(acc[:, h * HD:(h + 1) * HD], cos, sin).astype(jnp.bfloat16) for h in range(GROUP)]
    new_k = turn(acc[:, QW:QW + HD], cos, sin).astype(jnp.bfloat16).astype(jnp.float32)
    new_v = acc[:, QW + HD:].astype(jnp.bfloat16).astype(jnp.float32)
    arrived(CHUNKS)
    n = 8
    col = lax.broadcasted_iota(jnp.int32, (GROUP * n, n * ctx), 1)
    row = lax.broadcasted_iota(jnp.int32, (GROUP * n, n * ctx), 0)
    rel = col - (row % n) * ctx
    for g in range(rows // n):
        lo, hi = g * n, (g + 1) * n
        q = jnp.concatenate([h[lo:hi].astype(jnp.float32) for h in heads], axis=0)
        nk = jnp.concatenate([new_k[lo:hi]] * GROUP, axis=0)
        nv = jnp.concatenate([new_v[lo:hi]] * GROUP, axis=0)
        ln = jnp.concatenate([len_ref[lo:hi, :]] * GROUP, axis=0)
        keys = kc[pl.ds(lo, n)].reshape(n * ctx, HD)
        vals = vc[pl.ds(lo, n)].reshape(n * ctx, HD)
        s = lax.dot_general(
            q.astype(jnp.bfloat16), keys, (((1,), (1,)), ((), ())), preferred_element_type=jnp.float32
        )
        own = jnp.sum(q * nk, axis=1, keepdims=True)
        wt = jnp.exp(CAP * jnp.tanh(s * (SCALE / CAP)) - CAP)
        wt = jnp.where((rel >= 0) & (rel < ln), wt, 0.0)
        own_w = jnp.exp(CAP * jnp.tanh(own * (SCALE / CAP)) - CAP)
        total = jnp.sum(wt, axis=1, keepdims=True) + own_w
        probs = (wt / total).astype(jnp.bfloat16)
        own_p = (own_w / total).astype(jnp.bfloat16).astype(jnp.float32)
        mixed = jnp.dot(probs, vals, preferred_element_type=jnp.float32) + own_p * nv
        for h in range(GROUP):
            ho[pl.ds(lo, n), pl.ds(h * HD, HD)] = mixed[h * n:(h + 1) * n]
    arrived(CHUNKS + 1)
    lhs = ho[...].astype(jnp.bfloat16)
    for c in range(CHUNKS):
        at = pl.ds(c * DC, DC)
        out = jnp.dot(lhs, wo[:, at], preferred_element_type=jnp.float32).astype(jnp.bfloat16)
        for b in range(blocks):
            o_ref[b, :, at] = out[b * per:(b + 1) * per]


def layer_call(sel, x, per, pre, cos, sin, lens, here, there):
    wo, kc, vc = here[3:]
    rows = lens.shape[0]
    return pl.pallas_call(
        layer_kernel,
        out_shape=jax.ShapeDtypeStruct((rows // per, per, D), jnp.bfloat16),
        in_specs=[pl.BlockSpec(memory_space=pltpu.SMEM)] + [VMEM] * 5 + [ANY] * 12,
        out_specs=VMEM,
        scratch_shapes=[
            pltpu.VMEM((rows, D), jnp.bfloat16),
            pltpu.VMEM((D, QW + 2 * HD), jnp.bfloat16),
            pltpu.VMEM(wo.shape, jnp.bfloat16),
            pltpu.VMEM((rows,) + kc.shape[1:], jnp.bfloat16),
            pltpu.VMEM((rows,) + vc.shape[1:], jnp.bfloat16),
            pltpu.VMEM((rows, QW), jnp.float32),
            pltpu.SemaphoreType.DMA((3 * CHUNKS,)),
            pltpu.SemaphoreType.DMA((3,)),
        ],
        compiler_params=pltpu.CompilerParams(vmem_limit_bytes=32 << 20),
        name="layer",
    )(sel, x, pre, cos, sin, lens, *here, *there)


def combine_kernel(p_ref, x_ref, post_ref, steer_ref, o_ref):
    total = p_ref[0].astype(jnp.float32)
    for b in range(1, p_ref.shape[0]):
        total += p_ref[b].astype(jnp.float32)
    factor = lax.rsqrt(jnp.mean(total * total, axis=1, keepdims=True) + EPS)
    post = total * factor * post_ref[...]
    o_ref[...] = (x_ref[...].astype(jnp.float32) + post + steer_ref[...]).astype(jnp.bfloat16)


def combine_call(parts, x, post, steer):
    return pl.pallas_call(
        combine_kernel,
        out_shape=jax.ShapeDtypeStruct(x.shape, jnp.bfloat16),
        in_specs=[VMEM] * 4,
        out_specs=VMEM,
        compiler_params=pltpu.CompilerParams(vmem_limit_bytes=8 << 20),
        name="combine",
    )(parts, x, post, steer)


def swap(value, axis):
    return lax.all_to_all(value, axis, 0, 0, tiled=True)


def on_device(
    resid, pre_gain, post_gain, w_query, w_key, w_value, w_out, key_cache, value_cache,
    lengths, concept, steer_layer, strength, directions,
):
    sections = lax.axis_size("section")
    lanes = lax.axis_size("tensor")
    section = lax.axis_index("section")
    lane = lax.axis_index("tensor")
    batch, width = resid.shape
    planes, core, plane = sections // 2, section % 2, section // 2
    rows = batch * planes
    per = rows // lanes
    start = core * rows

    def shifted(value, target):
        pairs = [(s * lanes + t, target(s) * lanes + t) for s in range(sections) for t in range(lanes)]
        return lax.ppermute(value, ("section", "tensor"), pairs)

    def other(value):
        return shifted(value, lambda s: s ^ 1)

    def mine(value):
        return lax.dynamic_slice_in_dim(value, start, rows, 0)

    here = (w_query[0], w_key[0], w_value[0], w_out[0],
            key_cache.reshape(batch * sections, *key_cache.shape[3:]),
            value_cache.reshape(batch * sections, *value_cache.shape[3:]))
    there = tuple(other(value) for value in here)
    gains = jnp.concatenate([pre_gain, post_gain], axis=0)
    other_gains = other(gains)
    by_layer = [jnp.where(core == 0, gains, other_gains), jnp.where(core == 0, other_gains, gains)]

    lens = mine(lengths)
    half = HD // 2
    frequency = 10000.0 ** (-(jnp.arange(half, dtype=jnp.float32) * 2.0) / HD)
    angles = lens.astype(jnp.float32)[:, None] * frequency[None, :]
    cosine, sine = jnp.cos(angles), jnp.sin(angles)
    cos = jnp.concatenate([cosine, cosine], axis=1)
    sin = jnp.concatenate([-sine, sine], axis=1)
    lens = lens[:, None]

    everyone = swap(jnp.broadcast_to(resid[None], (sections, batch, width)), "section")
    ids = jnp.arange(directions.shape[0], dtype=jnp.int32)
    one_hot = (mine(concept)[:, None] == ids[None, :]).astype(jnp.bfloat16)
    picked = jnp.dot(one_hot, directions, preferred_element_type=jnp.float32).astype(jnp.bfloat16)
    state = mine(everyone.reshape(batch * sections, width))
    both = jnp.concatenate(
        [jnp.broadcast_to(state[None], (lanes, rows, width)), picked.reshape(lanes, per, width)], axis=1
    )
    both = swap(both, "tensor")
    x = lax.dynamic_slice_in_dim(both, lane * per, per, 1).transpose(1, 0, 2).reshape(per, D)
    vectors = both[:, rows:].transpose(1, 0, 2).reshape(per, D).astype(jnp.float32)
    row = start + lane * per
    strengths = lax.dynamic_slice_in_dim(strength, row, per, 0)
    layers = lax.dynamic_slice_in_dim(steer_layer, row, per, 0)
    steers = [
        (strengths * (layers == 2 * plane + k).astype(jnp.float32))[:, None] * vectors for k in range(2)
    ]

    def layer(k, x, full):
        sel = jnp.stack([jnp.where(core == k, 0, 1), core]).astype(jnp.int32)
        parts = layer_call(sel, full, per, by_layer[k][:1], cos, sin, lens, here, there)
        parts = swap(parts, "tensor")
        return combine_call(parts, x, by_layer[k][1:], steers[k])

    def gathered(x):
        return swap(jnp.broadcast_to(x[None], (lanes, per, D)), "tensor")

    def opening(x):
        x = layer(0, x, both)
        return layer(1, x, gathered(x))

    def pair(x):
        x = layer(0, x, gathered(x))
        return layer(1, x, gathered(x))

    def step(p, x):
        x = shifted(x, lambda s: (s + 2) % sections)
        return lax.cond(plane == p, pair, lambda v: v, x)

    x = lax.cond(plane == 0, opening, lambda v: v, x)
    x = lax.fori_loop(1, planes, step, x)
    pieces = swap(x.reshape(per, lanes, width).transpose(1, 0, 2), "tensor")
    pieces = pieces.reshape(planes, batch, width)
    out = swap(jnp.concatenate([pieces, pieces], axis=0), "section")
    return lax.dynamic_index_in_dim(out, sections - 2 + section // planes, 0, keepdims=False)


def solution(mesh):
    placed = (
        P("section", "tensor"),
        P("section", None),
        P("section", None),
        P("section", None, "tensor"),
        P("section", None, "tensor"),
        P("section", None, "tensor"),
        P("section", "tensor", None),
        P("section", None, "tensor", None, None),
        P("section", None, "tensor", None, None),
        P(),
        P(),
        P(),
        P(),
        P(None, "tensor"),
    )
    return jax.shard_map(
        on_device, mesh=mesh, in_specs=placed, out_specs=P("section", "tensor"), check_vma=False
    )
```

```python
import math

import jax
import jax.numpy as jnp
from jax import lax
from jax.experimental import pallas as pl
from jax.experimental.pallas import tpu as pltpu
from jax.sharding import PartitionSpec as P

D = 4608
HEADS = 32
KVH = 16
HD = 128
GROUP = HEADS // KVH
QW = GROUP * HD
CHUNKS = 6
DC = D // CHUNKS
EPS = 1e-06
CAP = 50.0
SCALE = float(D // HEADS) ** (-0.5)
VMEM = pl.BlockSpec(memory_space=pltpu.VMEM)
HBM = pl.BlockSpec(memory_space=pltpu.HBM)


def turn(v, cos, sin):
    return v * cos + pltpu.roll(v, HD // 2, 1) * sin


def load_kernel(
    sel_ref,
    wq_a, wk_a, wv_a, wo_a, kc_a, vc_a,
    wq_b, wk_b, wv_b, wo_b, kc_b, vc_b,
    w, wo, kc, vc, sem,
):
    rows = kc.shape[0]
    mine = pl.ds(pl.multiple_of(sel_ref[1] * rows, rows), rows)

    def copies(wq_hbm, wk_hbm, wv_hbm, wo_hbm, kc_hbm, vc_hbm):
        return [
            pltpu.make_async_copy(wq_hbm, w.at[:, pl.ds(0, QW)], sem.at[0]),
            pltpu.make_async_copy(wk_hbm, w.at[:, pl.ds(QW, HD)], sem.at[1]),
            pltpu.make_async_copy(wv_hbm, w.at[:, pl.ds(QW + HD, HD)], sem.at[2]),
            pltpu.make_async_copy(kc_hbm.at[mine], kc, sem.at[3]),
            pltpu.make_async_copy(vc_hbm.at[mine], vc, sem.at[4]),
            pltpu.make_async_copy(wo_hbm, wo, sem.at[5]),
        ]

    own = copies(wq_a, wk_a, wv_a, wo_a, kc_a, vc_a)

    @pl.when(sel_ref[0] == 0)
    def _():
        for copy in own:
            copy.start()

    @pl.when(sel_ref[0] != 0)
    def _():
        for copy in copies(wq_b, wk_b, wv_b, wo_b, kc_b, vc_b):
            copy.start()

    for copy in own:
        copy.wait()


def load_call(sel, rows, here, there):
    wo, kc, vc = here[3:]
    shapes = [(D, QW + 2 * HD), wo.shape, (rows,) + kc.shape[1:], (rows,) + vc.shape[1:]]
    size = sum(2 * math.prod(shape) for shape in shapes)
    return pl.pallas_call(
        load_kernel,
        out_shape=[jax.ShapeDtypeStruct(shape, jnp.bfloat16) for shape in shapes],
        in_specs=[pl.BlockSpec(memory_space=pltpu.SMEM)] + [HBM] * 12,
        out_specs=[VMEM] * 4,
        scratch_shapes=[pltpu.SemaphoreType.DMA((6,))],
        compiler_params=pltpu.CompilerParams(vmem_limit_bytes=12 << 20),
        cost_estimate=pl.CostEstimate(flops=0, bytes_accessed=size, transcendentals=0),
        name="load",
    )(sel, *here, *there)


def project(x_ref, pre_ref, cos_ref, sin_ref, len_ref, w, wo, kc, vc, o_ref, xs, ho, arrived):
    rows = xs.shape[0]
    ctx = kc.shape[1]
    blocks, per = o_ref.shape[0], o_ref.shape[1]
    if x_ref.shape[1] == per:
        for b in range(blocks):
            xs[pl.ds(b * per, per), :] = x_ref[b]
    else:
        width = x_ref.shape[2]
        for b in range(blocks):
            xs[:, pl.ds(b * width, width)] = x_ref[b, pl.ds(0, rows), :]
    acc = jnp.zeros((rows, QW + 2 * HD), jnp.float32)
    squares = jnp.zeros((rows, 1), jnp.float32)
    for c in range(CHUNKS):
        part = xs[:, pl.ds(c * DC, DC)].astype(jnp.float32)
        squares += jnp.sum(part * part, axis=1, keepdims=True)
        scaled = (part * pre_ref[:, pl.ds(c * DC, DC)]).astype(jnp.bfloat16)
        arrived(c)
        acc += jnp.dot(scaled, w[pl.ds(c * DC, DC), :], preferred_element_type=jnp.float32)
    acc = acc * lax.rsqrt(squares / D + EPS)
    cos, sin = cos_ref[...], sin_ref[...]
    heads = [turn(acc[:, h * HD:(h + 1) * HD], cos, sin).astype(jnp.bfloat16) for h in range(GROUP)]
    new_k = turn(acc[:, QW:QW + HD], cos, sin).astype(jnp.bfloat16).astype(jnp.float32)
    new_v = acc[:, QW + HD:].astype(jnp.bfloat16).astype(jnp.float32)
    arrived(CHUNKS)
    n = 8
    col = lax.broadcasted_iota(jnp.int32, (GROUP * n, n * ctx), 1)
    row = lax.broadcasted_iota(jnp.int32, (GROUP * n, n * ctx), 0)
    rel = col - (row % n) * ctx
    for g in range(rows // n):
        lo, hi = g * n, (g + 1) * n
        q = jnp.concatenate([h[lo:hi].astype(jnp.float32) for h in heads], axis=0)
        nk = jnp.concatenate([new_k[lo:hi]] * GROUP, axis=0)
        nv = jnp.concatenate([new_v[lo:hi]] * GROUP, axis=0)
        ln = jnp.concatenate([len_ref[lo:hi, :1]] * GROUP, axis=0)
        keys = kc[pl.ds(lo, n)].reshape(n * ctx, HD)
        vals = vc[pl.ds(lo, n)].reshape(n * ctx, HD)
        s = lax.dot_general(
            q.astype(jnp.bfloat16), keys, (((1,), (1,)), ((), ())), preferred_element_type=jnp.float32
        )
        own = jnp.sum(q * nk, axis=1, keepdims=True)
        wt = jnp.exp(CAP * jnp.tanh(s * (SCALE / CAP)) - CAP)
        wt = jnp.where((rel >= 0) & (rel < ln), wt, 0.0)
        own_w = jnp.exp(CAP * jnp.tanh(own * (SCALE / CAP)) - CAP)
        total = jnp.sum(wt, axis=1, keepdims=True) + own_w
        probs = (wt / total).astype(jnp.bfloat16)
        own_p = (own_w / total).astype(jnp.bfloat16).astype(jnp.float32)
        mixed = jnp.dot(probs, vals, preferred_element_type=jnp.float32) + own_p * nv
        for h in range(GROUP):
            ho[pl.ds(lo, n), pl.ds(h * HD, HD)] = mixed[h * n:(h + 1) * n]
    arrived(CHUNKS + 1)
    lhs = ho[...].astype(jnp.bfloat16)
    for c in range(CHUNKS):
        at = pl.ds(c * DC, DC)
        out = jnp.dot(lhs, wo[:, at], preferred_element_type=jnp.float32).astype(jnp.bfloat16)
        for b in range(blocks):
            o_ref[b, :, at] = out[b * per:(b + 1) * per]


def layer_kernel(x_ref, pre_ref, cos_ref, sin_ref, len_ref, w, wo, kc, vc, o_ref, xs, ho):
    project(x_ref, pre_ref, cos_ref, sin_ref, len_ref, w, wo, kc, vc, o_ref, xs, ho, lambda step: None)


def opening_kernel(
    sel_ref, x_ref, pre_ref, cos_ref, sin_ref, len_ref,
    wq_a, wk_a, wv_a, wo_a, kc_a, vc_a,
    wq_b, wk_b, wv_b, wo_b, kc_b, vc_b,
    o_ref,
    xs, w, wo, kc, vc, ho, wsem, sem,
):
    rows = xs.shape[0]
    mine = pl.ds(pl.multiple_of(sel_ref[1] * rows, rows), rows)

    def copies(wq_hbm, wk_hbm, wv_hbm, wo_hbm, kc_hbm, vc_hbm):
        steps = []
        for c in range(CHUNKS):
            at = pl.ds(c * DC, DC)
            steps.append([
                pltpu.make_async_copy(wq_hbm.at[at], w.at[at, pl.ds(0, QW)], wsem.at[3 * c]),
                pltpu.make_async_copy(wk_hbm.at[at], w.at[at, pl.ds(QW, HD)], wsem.at[3 * c + 1]),
                pltpu.make_async_copy(wv_hbm.at[at], w.at[at, pl.ds(QW + HD, HD)], wsem.at[3 * c + 2]),
            ])
        steps.append([
            pltpu.make_async_copy(kc_hbm.at[mine], kc, sem.at[0]),
            pltpu.make_async_copy(vc_hbm.at[mine], vc, sem.at[1]),
        ])
        steps.append([pltpu.make_async_copy(wo_hbm, wo, sem.at[2])])
        return steps

    def begin(steps):
        for step in steps:
            for copy in step:
                copy.start()

    first = copies(wq_a, wk_a, wv_a, wo_a, kc_a, vc_a)

    @pl.when(sel_ref[0] == 0)
    def _():
        begin(first)

    @pl.when(sel_ref[0] != 0)
    def _():
        begin(copies(wq_b, wk_b, wv_b, wo_b, kc_b, vc_b))

    def arrived(step):
        for copy in first[step]:
            copy.wait()

    project(x_ref, pre_ref, cos_ref, sin_ref, len_ref, w, wo, kc, vc, o_ref, xs, ho, arrived)


def opening_call(sel, x, per, pre, cos, sin, lens, here, there):
    wo, kc, vc = here[3:]
    rows = lens.shape[0]
    return pl.pallas_call(
        opening_kernel,
        out_shape=jax.ShapeDtypeStruct((rows // per, per, D), jnp.bfloat16),
        in_specs=[pl.BlockSpec(memory_space=pltpu.SMEM)] + [VMEM] * 5 + [HBM] * 12,
        out_specs=VMEM,
        scratch_shapes=[
            pltpu.VMEM((rows, D), jnp.bfloat16),
            pltpu.VMEM((D, QW + 2 * HD), jnp.bfloat16),
            pltpu.VMEM(wo.shape, jnp.bfloat16),
            pltpu.VMEM((rows,) + kc.shape[1:], jnp.bfloat16),
            pltpu.VMEM((rows,) + vc.shape[1:], jnp.bfloat16),
            pltpu.VMEM((rows, QW), jnp.float32),
            pltpu.SemaphoreType.DMA((3 * CHUNKS,)),
            pltpu.SemaphoreType.DMA((3,)),
        ],
        compiler_params=pltpu.CompilerParams(vmem_limit_bytes=32 << 20),
        name="opening",
    )(sel, x, pre, cos, sin, lens, *here, *there)


def layer_call(x, per, pre, cos, sin, lens, loaded):
    rows = lens.shape[0]
    return pl.pallas_call(
        layer_kernel,
        out_shape=jax.ShapeDtypeStruct((rows // per, per, D), jnp.bfloat16),
        in_specs=[VMEM] * 9,
        out_specs=VMEM,
        scratch_shapes=[pltpu.VMEM((rows, D), jnp.bfloat16), pltpu.VMEM((rows, QW), jnp.float32)],
        compiler_params=pltpu.CompilerParams(vmem_limit_bytes=14 << 20),
        name="layer",
    )(x, pre, cos, sin, lens, *loaded)


def combine_kernel(p_ref, x_ref, post_ref, steer_ref, o_ref):
    total = p_ref[0].astype(jnp.float32)
    for b in range(1, p_ref.shape[0]):
        total += p_ref[b].astype(jnp.float32)
    factor = lax.rsqrt(jnp.mean(total * total, axis=1, keepdims=True) + EPS)
    post = total * factor * post_ref[...]
    o_ref[...] = (x_ref[...].astype(jnp.float32) + post + steer_ref[...]).astype(jnp.bfloat16)


def combine_call(parts, x, post, steer):
    return pl.pallas_call(
        combine_kernel,
        out_shape=jax.ShapeDtypeStruct(x.shape, jnp.bfloat16),
        in_specs=[VMEM] * 4,
        out_specs=VMEM,
        compiler_params=pltpu.CompilerParams(vmem_limit_bytes=8 << 20),
        name="combine",
    )(parts, x, post, steer)


def swap(value, axis):
    return lax.all_to_all(value, axis, 0, 0, tiled=True)


def on_device(
    resid, pre_gain, post_gain, w_query, w_key, w_value, w_out, key_cache, value_cache,
    lengths, concept, steer_layer, strength, directions,
):
    sections = lax.axis_size("section")
    lanes = lax.axis_size("tensor")
    section = lax.axis_index("section")
    lane = lax.axis_index("tensor")
    batch, width = resid.shape
    planes, core, plane = sections // 2, section % 2, section // 2
    rows = batch * planes
    per = rows // lanes
    start = core * rows

    def shifted(value, target):
        pairs = [(s * lanes + t, target(s) * lanes + t) for s in range(sections) for t in range(lanes)]
        return lax.ppermute(value, ("section", "tensor"), pairs)

    def other(value):
        return shifted(value, lambda s: s ^ 1)

    def mine(value):
        return lax.dynamic_slice_in_dim(value, start, rows, 0)

    here = (w_query[0], w_key[0], w_value[0], w_out[0],
            key_cache.reshape(batch * sections, *key_cache.shape[3:]),
            value_cache.reshape(batch * sections, *value_cache.shape[3:]))
    there = tuple(other(value) for value in here)
    gains = jnp.concatenate([pre_gain, post_gain], axis=0)
    other_gains = other(gains)
    by_layer = [jnp.where(core == 0, gains, other_gains), jnp.where(core == 0, other_gains, gains)]

    lens = mine(lengths)
    half = HD // 2
    frequency = 10000.0 ** (-(jnp.arange(half, dtype=jnp.float32) * 2.0) / HD)
    angles = lens.astype(jnp.float32)[:, None] * frequency[None, :]
    cosine, sine = jnp.cos(angles), jnp.sin(angles)
    cos = jnp.concatenate([cosine, cosine], axis=1)
    sin = jnp.concatenate([-sine, sine], axis=1)
    lens = jnp.broadcast_to(lens[:, None], (rows, HD))

    everyone = swap(jnp.broadcast_to(resid[None], (sections, batch, width)), "section")
    ids = jnp.arange(directions.shape[0], dtype=jnp.int32)
    one_hot = (mine(concept)[:, None] == ids[None, :]).astype(jnp.bfloat16)
    picked = jnp.dot(one_hot, directions, preferred_element_type=jnp.float32).astype(jnp.bfloat16)
    state = mine(everyone.reshape(batch * sections, width))
    both = jnp.concatenate(
        [jnp.broadcast_to(state[None], (lanes, rows, width)), picked.reshape(lanes, per, width)], axis=1
    )
    both = swap(both, "tensor")
    x = lax.dynamic_slice_in_dim(both, lane * per, per, 1).transpose(1, 0, 2).reshape(per, D)
    vectors = both[:, rows:].transpose(1, 0, 2).reshape(per, D).astype(jnp.float32)
    row = start + lane * per
    strengths = lax.dynamic_slice_in_dim(strength, row, per, 0)
    layers = lax.dynamic_slice_in_dim(steer_layer, row, per, 0)
    steers = [
        (strengths * (layers == 2 * plane + k).astype(jnp.float32))[:, None] * vectors for k in range(2)
    ]

    sels = [jnp.stack([jnp.where(core == k, 0, 1), core]).astype(jnp.int32) for k in range(2)]
    pre = [value[:1] for value in by_layer]
    post = [value[1:] for value in by_layer]
    cos, sin, lens, pre, post, steers, sels = lax.optimization_barrier(
        (cos, sin, lens, pre, post, steers, sels)
    )

    def finish(k, x, parts):
        return combine_call(swap(parts, "tensor"), x, post[k], steers[k])

    def gathered(x):
        return swap(jnp.broadcast_to(x[None], (lanes, per, D)), "tensor")

    def opening(x):
        full = both
        for k in range(2):
            x = finish(k, x, opening_call(sels[k], full, per, pre[k], cos, sin, lens, here, there))
            full = gathered(x) if k == 0 else None
        return x

    x = lax.cond(plane == 0, opening, lambda v: v, x)
    x, late = lax.optimization_barrier((x, sels))
    loaded = [load_call(late[k], rows, here, there) for k in range(2)]

    def pair(x):
        for k in range(2):
            x = finish(k, x, layer_call(gathered(x), per, pre[k], cos, sin, lens, loaded[k]))
        return x

    for p in range(1, planes):
        x = shifted(x, lambda s: (s + 2) % sections)
        x = lax.cond(plane == p, pair, lambda v: v, x)
    pieces = swap(x.reshape(per, lanes, width).transpose(1, 0, 2), "tensor")
    pieces = pieces.reshape(planes, batch, width)
    out = swap(jnp.concatenate([pieces, pieces], axis=0), "section")
    return lax.dynamic_index_in_dim(out, sections - 2 + section // planes, 0, keepdims=False)


def solution(mesh):
    placed = (
        P("section", "tensor"),
        P("section", None),
        P("section", None),
        P("section", None, "tensor"),
        P("section", None, "tensor"),
        P("section", None, "tensor"),
        P("section", "tensor", None),
        P("section", None, "tensor", None, None),
        P("section", None, "tensor", None, None),
        P(),
        P(),
        P(),
        P(),
        P(None, "tensor"),
    )
    return jax.shard_map(
        on_device, mesh=mesh, in_specs=placed, out_specs=P("section", "tensor"), check_vma=False
    )
```

```python
import math

import jax
import jax.numpy as jnp
from jax import lax
from jax.experimental import pallas as pl
from jax.experimental.pallas import tpu as pltpu
from jax.sharding import PartitionSpec as P

D = 4608
HEADS = 32
KVH = 16
HD = 128
GROUP = HEADS // KVH
QW = GROUP * HD
CHUNKS = 6
DC = D // CHUNKS
EPS = 1e-06
CAP = 50.0
SCALE = float(D // HEADS) ** (-0.5)
VMEM = pl.BlockSpec(memory_space=pltpu.VMEM)
HBM = pl.BlockSpec(memory_space=pltpu.HBM)


def turn(v, cos, sin):
    return v * cos + pltpu.roll(v, HD // 2, 1) * sin


def load_kernel(
    sel_ref,
    wq_a, wk_a, wv_a, wo_a, kc_a, vc_a,
    wq_b, wk_b, wv_b, wo_b, kc_b, vc_b,
    w, wo, kc, vc, sem,
):
    rows = kc.shape[0]
    mine = pl.ds(pl.multiple_of(sel_ref[1] * rows, rows), rows)

    def copies(wq_hbm, wk_hbm, wv_hbm, wo_hbm, kc_hbm, vc_hbm):
        return [
            pltpu.make_async_copy(wq_hbm, w.at[:, pl.ds(0, QW)], sem.at[0]),
            pltpu.make_async_copy(wk_hbm, w.at[:, pl.ds(QW, HD)], sem.at[1]),
            pltpu.make_async_copy(wv_hbm, w.at[:, pl.ds(QW + HD, HD)], sem.at[2]),
            pltpu.make_async_copy(kc_hbm.at[mine], kc, sem.at[3]),
            pltpu.make_async_copy(vc_hbm.at[mine], vc, sem.at[4]),
            pltpu.make_async_copy(wo_hbm, wo, sem.at[5]),
        ]

    own = copies(wq_a, wk_a, wv_a, wo_a, kc_a, vc_a)

    @pl.when(sel_ref[0] == 0)
    def _():
        for copy in own:
            copy.start()

    @pl.when(sel_ref[0] != 0)
    def _():
        for copy in copies(wq_b, wk_b, wv_b, wo_b, kc_b, vc_b):
            copy.start()

    for copy in own:
        copy.wait()


def load_call(sel, rows, here, there):
    wo, kc, vc = here[3:]
    shapes = [(D, QW + 2 * HD), wo.shape, (rows,) + kc.shape[1:], (rows,) + vc.shape[1:]]
    size = sum(2 * math.prod(shape) for shape in shapes)
    return pl.pallas_call(
        load_kernel,
        out_shape=[jax.ShapeDtypeStruct(shape, jnp.bfloat16) for shape in shapes],
        in_specs=[pl.BlockSpec(memory_space=pltpu.SMEM)] + [HBM] * 12,
        out_specs=[VMEM] * 4,
        scratch_shapes=[pltpu.SemaphoreType.DMA((6,))],
        compiler_params=pltpu.CompilerParams(vmem_limit_bytes=12 << 20),
        cost_estimate=pl.CostEstimate(flops=0, bytes_accessed=size, transcendentals=0),
        name="load",
    )(sel, *here, *there)


def layer_kernel(x_ref, pre_ref, cos_ref, sin_ref, len_ref, w, wo, kc, vc, o_ref, xs, ho):
    rows = xs.shape[0]
    ctx = kc.shape[1]
    blocks, per = o_ref.shape[0], o_ref.shape[1]
    if x_ref.shape[1] == per:
        for b in range(blocks):
            xs[pl.ds(b * per, per), :] = x_ref[b]
    else:
        width = x_ref.shape[2]
        for b in range(blocks):
            xs[:, pl.ds(b * width, width)] = x_ref[b, pl.ds(0, rows), :]
    acc = jnp.zeros((rows, QW + 2 * HD), jnp.float32)
    squares = jnp.zeros((rows, 1), jnp.float32)
    for c in range(CHUNKS):
        part = xs[:, pl.ds(c * DC, DC)].astype(jnp.float32)
        squares += jnp.sum(part * part, axis=1, keepdims=True)
        scaled = (part * pre_ref[:, pl.ds(c * DC, DC)]).astype(jnp.bfloat16)
        acc += jnp.dot(scaled, w[pl.ds(c * DC, DC), :], preferred_element_type=jnp.float32)
    acc = acc * lax.rsqrt(squares / D + EPS)
    cos, sin = cos_ref[...], sin_ref[...]
    heads = [turn(acc[:, h * HD:(h + 1) * HD], cos, sin).astype(jnp.bfloat16) for h in range(GROUP)]
    new_k = turn(acc[:, QW:QW + HD], cos, sin).astype(jnp.bfloat16).astype(jnp.float32)
    new_v = acc[:, QW + HD:].astype(jnp.bfloat16).astype(jnp.float32)
    n = 8
    col = lax.broadcasted_iota(jnp.int32, (GROUP * n, n * ctx), 1)
    row = lax.broadcasted_iota(jnp.int32, (GROUP * n, n * ctx), 0)
    rel = col - (row % n) * ctx
    for g in range(rows // n):
        lo, hi = g * n, (g + 1) * n
        q = jnp.concatenate([h[lo:hi].astype(jnp.float32) for h in heads], axis=0)
        nk = jnp.concatenate([new_k[lo:hi]] * GROUP, axis=0)
        nv = jnp.concatenate([new_v[lo:hi]] * GROUP, axis=0)
        ln = jnp.concatenate([len_ref[lo:hi, :1]] * GROUP, axis=0)
        keys = kc[pl.ds(lo, n)].reshape(n * ctx, HD)
        vals = vc[pl.ds(lo, n)].reshape(n * ctx, HD)
        s = lax.dot_general(
            q.astype(jnp.bfloat16), keys, (((1,), (1,)), ((), ())), preferred_element_type=jnp.float32
        )
        own = jnp.sum(q * nk, axis=1, keepdims=True)
        wt = jnp.exp(CAP * jnp.tanh(s * (SCALE / CAP)) - CAP)
        wt = jnp.where((rel >= 0) & (rel < ln), wt, 0.0)
        own_w = jnp.exp(CAP * jnp.tanh(own * (SCALE / CAP)) - CAP)
        total = jnp.sum(wt, axis=1, keepdims=True) + own_w
        probs = (wt / total).astype(jnp.bfloat16)
        own_p = (own_w / total).astype(jnp.bfloat16).astype(jnp.float32)
        mixed = jnp.dot(probs, vals, preferred_element_type=jnp.float32) + own_p * nv
        for h in range(GROUP):
            ho[pl.ds(lo, n), pl.ds(h * HD, HD)] = mixed[h * n:(h + 1) * n]
    lhs = ho[...].astype(jnp.bfloat16)
    for c in range(CHUNKS):
        at = pl.ds(c * DC, DC)
        out = jnp.dot(lhs, wo[:, at], preferred_element_type=jnp.float32).astype(jnp.bfloat16)
        for b in range(blocks):
            o_ref[b, :, at] = out[b * per:(b + 1) * per]


def layer_call(x, per, pre, cos, sin, lens, loaded):
    rows = lens.shape[0]
    return pl.pallas_call(
        layer_kernel,
        out_shape=jax.ShapeDtypeStruct((rows // per, per, D), jnp.bfloat16),
        in_specs=[VMEM] * 9,
        out_specs=VMEM,
        scratch_shapes=[pltpu.VMEM((rows, D), jnp.bfloat16), pltpu.VMEM((rows, QW), jnp.float32)],
        compiler_params=pltpu.CompilerParams(vmem_limit_bytes=14 << 20),
        name="layer",
    )(x, pre, cos, sin, lens, *loaded)


def combine_kernel(p_ref, x_ref, post_ref, steer_ref, o_ref):
    total = p_ref[0].astype(jnp.float32)
    for b in range(1, p_ref.shape[0]):
        total += p_ref[b].astype(jnp.float32)
    factor = lax.rsqrt(jnp.mean(total * total, axis=1, keepdims=True) + EPS)
    post = total * factor * post_ref[...]
    o_ref[...] = (x_ref[...].astype(jnp.float32) + post + steer_ref[...]).astype(jnp.bfloat16)


def combine_call(parts, x, post, steer):
    return pl.pallas_call(
        combine_kernel,
        out_shape=jax.ShapeDtypeStruct(x.shape, jnp.bfloat16),
        in_specs=[VMEM] * 4,
        out_specs=VMEM,
        compiler_params=pltpu.CompilerParams(vmem_limit_bytes=8 << 20),
        name="combine",
    )(parts, x, post, steer)


def swap(value, axis):
    return lax.all_to_all(value, axis, 0, 0, tiled=True)


def on_device(
    resid, pre_gain, post_gain, w_query, w_key, w_value, w_out, key_cache, value_cache,
    lengths, concept, steer_layer, strength, directions,
):
    sections = lax.axis_size("section")
    lanes = lax.axis_size("tensor")
    section = lax.axis_index("section")
    lane = lax.axis_index("tensor")
    batch, width = resid.shape
    planes, core, plane = sections // 2, section % 2, section // 2
    rows = batch * planes
    per = rows // lanes
    start = core * rows

    def shifted(value, target):
        pairs = [(s * lanes + t, target(s) * lanes + t) for s in range(sections) for t in range(lanes)]
        return lax.ppermute(value, ("section", "tensor"), pairs)

    def other(value):
        return shifted(value, lambda s: s ^ 1)

    def mine(value):
        return lax.dynamic_slice_in_dim(value, start, rows, 0)

    here = (w_query[0], w_key[0], w_value[0], w_out[0],
            key_cache.reshape(batch * sections, *key_cache.shape[3:]),
            value_cache.reshape(batch * sections, *value_cache.shape[3:]))
    here = tuple(pltpu.with_memory_space_constraint(value, pltpu.HBM) for value in here)
    there = tuple(pltpu.with_memory_space_constraint(other(value), pltpu.HBM) for value in here)
    gains = jnp.concatenate([pre_gain, post_gain], axis=0)
    other_gains = other(gains)
    by_layer = [jnp.where(core == 0, gains, other_gains), jnp.where(core == 0, other_gains, gains)]

    lens = mine(lengths)
    half = HD // 2
    frequency = 10000.0 ** (-(jnp.arange(half, dtype=jnp.float32) * 2.0) / HD)
    angles = lens.astype(jnp.float32)[:, None] * frequency[None, :]
    cosine, sine = jnp.cos(angles), jnp.sin(angles)
    cos = jnp.concatenate([cosine, cosine], axis=1)
    sin = jnp.concatenate([-sine, sine], axis=1)
    lens = jnp.broadcast_to(lens[:, None], (rows, HD))

    everyone = swap(jnp.broadcast_to(resid[None], (sections, batch, width)), "section")
    ids = jnp.arange(directions.shape[0], dtype=jnp.int32)
    one_hot = (mine(concept)[:, None] == ids[None, :]).astype(jnp.bfloat16)
    picked = jnp.dot(one_hot, directions, preferred_element_type=jnp.float32).astype(jnp.bfloat16)
    state = mine(everyone.reshape(batch * sections, width))
    both = jnp.concatenate(
        [jnp.broadcast_to(state[None], (lanes, rows, width)), picked.reshape(lanes, per, width)], axis=1
    )
    both = swap(both, "tensor")
    x = lax.dynamic_slice_in_dim(both, lane * per, per, 1).transpose(1, 0, 2).reshape(per, D)
    vectors = both[:, rows:].transpose(1, 0, 2).reshape(per, D).astype(jnp.float32)
    row = start + lane * per
    strengths = lax.dynamic_slice_in_dim(strength, row, per, 0)
    layers = lax.dynamic_slice_in_dim(steer_layer, row, per, 0)
    steers = [
        (strengths * (layers == 2 * plane + k).astype(jnp.float32))[:, None] * vectors for k in range(2)
    ]

    sels = [jnp.stack([jnp.where(core == k, 0, 1), core]).astype(jnp.int32) for k in range(2)]
    pre = [value[:1] for value in by_layer]
    post = [value[1:] for value in by_layer]
    cos, sin, lens, pre, post, steers, sels = lax.optimization_barrier(
        (cos, sin, lens, pre, post, steers, sels)
    )

    def gathered(x):
        return swap(jnp.broadcast_to(x[None], (lanes, per, D)), "tensor")

    loaded = [load_call(sels[k], rows, here, there) for k in range(2)]
    x, both, loaded = lax.optimization_barrier((x, both, loaded))
    for p in range(planes):
        if p:
            x = shifted(x, lambda s: (s + 2) % sections)
        for k in range(2):
            full = gathered(x) if p or k else both
            parts = layer_call(full, per, pre[k], cos, sin, lens, loaded[k])
            x = combine_call(swap(parts, "tensor"), x, post[k], steers[k])
    pieces = swap(x.reshape(per, lanes, width).transpose(1, 0, 2), "tensor")
    pieces = pieces.reshape(planes, batch, width)
    out = swap(jnp.concatenate([pieces, pieces], axis=0), "section")
    return lax.dynamic_index_in_dim(out, sections - 2 + section // planes, 0, keepdims=False)


def solution(mesh):
    placed = (
        P("section", "tensor"),
        P("section", None),
        P("section", None),
        P("section", None, "tensor"),
        P("section", None, "tensor"),
        P("section", None, "tensor"),
        P("section", "tensor", None),
        P("section", None, "tensor", None, None),
        P("section", None, "tensor", None, None),
        P(),
        P(),
        P(),
        P(),
        P(None, "tensor"),
    )
    return jax.shard_map(
        on_device, mesh=mesh, in_specs=placed, out_specs=P("section", "tensor"), check_vma=False
    )
```

```python
import jax
import jax.numpy as jnp
from jax import lax
from jax.experimental import pallas as pl
from jax.experimental.pallas import tpu as pltpu
from jax.sharding import PartitionSpec as P

D = 4608
HEADS = 32
KVH = 16
HD = 128
GROUP = HEADS // KVH
QW = GROUP * HD
CHUNKS = 6
DC = D // CHUNKS
EPS = 1e-06
CAP = 50.0
SCALE = float(D // HEADS) ** (-0.5)
VMEM = pl.BlockSpec(memory_space=pltpu.VMEM)
ANY = pl.BlockSpec(memory_space=pl.ANY)


def turn(v, cos, sin):
    return v * cos + pltpu.roll(v, HD // 2, 1) * sin


def project(x_ref, pre_ref, cos_ref, sin_ref, len_ref, w, wo, kc, vc, o_ref, xs, ho, arrived):
    rows = xs.shape[0]
    ctx = kc.shape[1]
    blocks, per = o_ref.shape[0], o_ref.shape[1]
    if x_ref.shape[1] == per:
        for b in range(blocks):
            xs[pl.ds(b * per, per), :] = x_ref[b]
    else:
        width = x_ref.shape[2]
        for b in range(blocks):
            xs[:, pl.ds(b * width, width)] = x_ref[b, pl.ds(0, rows), :]
    acc = jnp.zeros((rows, QW + 2 * HD), jnp.float32)
    squares = jnp.zeros((rows, 1), jnp.float32)
    for c in range(CHUNKS):
        part = xs[:, pl.ds(c * DC, DC)].astype(jnp.float32)
        squares += jnp.sum(part * part, axis=1, keepdims=True)
        scaled = (part * pre_ref[:, pl.ds(c * DC, DC)]).astype(jnp.bfloat16)
        arrived(c)
        acc += jnp.dot(scaled, w[pl.ds(c * DC, DC), :], preferred_element_type=jnp.float32)
    acc = acc * lax.rsqrt(squares / D + EPS)
    cos, sin = cos_ref[...], sin_ref[...]
    heads = [turn(acc[:, h * HD:(h + 1) * HD], cos, sin).astype(jnp.bfloat16) for h in range(GROUP)]
    new_k = turn(acc[:, QW:QW + HD], cos, sin).astype(jnp.bfloat16).astype(jnp.float32)
    new_v = acc[:, QW + HD:].astype(jnp.bfloat16).astype(jnp.float32)
    arrived(CHUNKS)
    n = 8
    col = lax.broadcasted_iota(jnp.int32, (GROUP * n, n * ctx), 1)
    row = lax.broadcasted_iota(jnp.int32, (GROUP * n, n * ctx), 0)
    rel = col - (row % n) * ctx
    for g in range(rows // n):
        lo, hi = g * n, (g + 1) * n
        q = jnp.concatenate([h[lo:hi].astype(jnp.float32) for h in heads], axis=0)
        nk = jnp.concatenate([new_k[lo:hi]] * GROUP, axis=0)
        nv = jnp.concatenate([new_v[lo:hi]] * GROUP, axis=0)
        ln = jnp.concatenate([len_ref[lo:hi, :1]] * GROUP, axis=0)
        keys = kc[pl.ds(lo, n)].reshape(n * ctx, HD)
        vals = vc[pl.ds(lo, n)].reshape(n * ctx, HD)
        s = lax.dot_general(
            q.astype(jnp.bfloat16), keys, (((1,), (1,)), ((), ())), preferred_element_type=jnp.float32
        )
        own = jnp.sum(q * nk, axis=1, keepdims=True)
        wt = jnp.exp(CAP * jnp.tanh(s * (SCALE / CAP)) - CAP)
        wt = jnp.where((rel >= 0) & (rel < ln), wt, 0.0)
        own_w = jnp.exp(CAP * jnp.tanh(own * (SCALE / CAP)) - CAP)
        total = jnp.sum(wt, axis=1, keepdims=True) + own_w
        probs = (wt / total).astype(jnp.bfloat16)
        own_p = (own_w / total).astype(jnp.bfloat16).astype(jnp.float32)
        mixed = jnp.dot(probs, vals, preferred_element_type=jnp.float32) + own_p * nv
        for h in range(GROUP):
            ho[pl.ds(lo, n), pl.ds(h * HD, HD)] = mixed[h * n:(h + 1) * n]
    arrived(CHUNKS + 1)
    lhs = ho[...].astype(jnp.bfloat16)
    for c in range(CHUNKS):
        at = pl.ds(c * DC, DC)
        out = jnp.dot(lhs, wo[:, at], preferred_element_type=jnp.float32).astype(jnp.bfloat16)
        for b in range(blocks):
            o_ref[b, :, at] = out[b * per:(b + 1) * per]


def layer_kernel(x_ref, pre_ref, cos_ref, sin_ref, len_ref, w, wo, kc, vc, o_ref, xs, ho):
    project(x_ref, pre_ref, cos_ref, sin_ref, len_ref, w, wo, kc, vc, o_ref, xs, ho, lambda step: None)


def opening_kernel(
    sel_ref, x_ref, pre_ref, cos_ref, sin_ref, len_ref,
    wq_a, wk_a, wv_a, wo_a, kc_a, vc_a,
    wq_b, wk_b, wv_b, wo_b, kc_b, vc_b,
    o_ref, w, wo, kc, vc,
    xs, ho, wsem, sem,
):
    rows = xs.shape[0]
    mine = pl.ds(pl.multiple_of(sel_ref[1] * rows, rows), rows)

    def copies(wq_hbm, wk_hbm, wv_hbm, wo_hbm, kc_hbm, vc_hbm):
        steps = []
        for c in range(CHUNKS):
            at = pl.ds(c * DC, DC)
            steps.append([
                pltpu.make_async_copy(wq_hbm.at[at], w.at[at, pl.ds(0, QW)], wsem.at[3 * c]),
                pltpu.make_async_copy(wk_hbm.at[at], w.at[at, pl.ds(QW, HD)], wsem.at[3 * c + 1]),
                pltpu.make_async_copy(wv_hbm.at[at], w.at[at, pl.ds(QW + HD, HD)], wsem.at[3 * c + 2]),
            ])
        steps.append([
            pltpu.make_async_copy(kc_hbm.at[mine], kc, sem.at[0]),
            pltpu.make_async_copy(vc_hbm.at[mine], vc, sem.at[1]),
        ])
        steps.append([pltpu.make_async_copy(wo_hbm, wo, sem.at[2])])
        return steps

    def begin(steps):
        for step in steps:
            for copy in step:
                copy.start()

    first = copies(wq_a, wk_a, wv_a, wo_a, kc_a, vc_a)

    @pl.when(sel_ref[0] == 0)
    def _():
        begin(first)

    @pl.when(sel_ref[0] != 0)
    def _():
        begin(copies(wq_b, wk_b, wv_b, wo_b, kc_b, vc_b))

    def arrived(step):
        for copy in first[step]:
            copy.wait()

    project(x_ref, pre_ref, cos_ref, sin_ref, len_ref, w, wo, kc, vc, o_ref, xs, ho, arrived)


def opening_call(sel, x, per, pre, cos, sin, lens, here, there):
    wo, kc, vc = here[3:]
    rows = lens.shape[0]
    shapes = [(rows // per, per, D), (D, QW + 2 * HD), wo.shape, (rows,) + kc.shape[1:], (rows,) + vc.shape[1:]]
    out, *loaded = pl.pallas_call(
        opening_kernel,
        out_shape=[jax.ShapeDtypeStruct(shape, jnp.bfloat16) for shape in shapes],
        in_specs=[pl.BlockSpec(memory_space=pltpu.SMEM)] + [VMEM] * 5 + [ANY] * 12,
        out_specs=[VMEM] * 5,
        scratch_shapes=[
            pltpu.VMEM((rows, D), jnp.bfloat16),
            pltpu.VMEM((rows, QW), jnp.float32),
            pltpu.SemaphoreType.DMA((3 * CHUNKS,)),
            pltpu.SemaphoreType.DMA((3,)),
        ],
        compiler_params=pltpu.CompilerParams(vmem_limit_bytes=24 << 20),
        name="opening",
    )(sel, x, pre, cos, sin, lens, *here, *there)
    return out, loaded


def layer_call(x, per, pre, cos, sin, lens, loaded):
    rows = lens.shape[0]
    return pl.pallas_call(
        layer_kernel,
        out_shape=jax.ShapeDtypeStruct((rows // per, per, D), jnp.bfloat16),
        in_specs=[VMEM] * 9,
        out_specs=VMEM,
        scratch_shapes=[pltpu.VMEM((rows, D), jnp.bfloat16), pltpu.VMEM((rows, QW), jnp.float32)],
        compiler_params=pltpu.CompilerParams(vmem_limit_bytes=14 << 20),
        name="layer",
    )(x, pre, cos, sin, lens, *loaded)


def combine_kernel(p_ref, x_ref, post_ref, steer_ref, o_ref):
    total = p_ref[0].astype(jnp.float32)
    for b in range(1, p_ref.shape[0]):
        total += p_ref[b].astype(jnp.float32)
    factor = lax.rsqrt(jnp.mean(total * total, axis=1, keepdims=True) + EPS)
    post = total * factor * post_ref[...]
    o_ref[...] = (x_ref[...].astype(jnp.float32) + post + steer_ref[...]).astype(jnp.bfloat16)


def combine_call(parts, x, post, steer):
    return pl.pallas_call(
        combine_kernel,
        out_shape=jax.ShapeDtypeStruct(x.shape, jnp.bfloat16),
        in_specs=[VMEM] * 4,
        out_specs=VMEM,
        compiler_params=pltpu.CompilerParams(vmem_limit_bytes=8 << 20),
        name="combine",
    )(parts, x, post, steer)


def swap(value, axis):
    return lax.all_to_all(value, axis, 0, 0, tiled=True)


def on_device(
    resid, pre_gain, post_gain, w_query, w_key, w_value, w_out, key_cache, value_cache,
    lengths, concept, steer_layer, strength, directions,
):
    sections = lax.axis_size("section")
    lanes = lax.axis_size("tensor")
    section = lax.axis_index("section")
    lane = lax.axis_index("tensor")
    batch, width = resid.shape
    planes, core, plane = sections // 2, section % 2, section // 2
    rows = batch * planes
    per = rows // lanes
    start = core * rows

    def shifted(value, target):
        pairs = [(s * lanes + t, target(s) * lanes + t) for s in range(sections) for t in range(lanes)]
        return lax.ppermute(value, ("section", "tensor"), pairs)

    def other(value):
        return shifted(value, lambda s: s ^ 1)

    def mine(value):
        return lax.dynamic_slice_in_dim(value, start, rows, 0)

    here = (w_query[0], w_key[0], w_value[0], w_out[0],
            key_cache.reshape(batch * sections, *key_cache.shape[3:]),
            value_cache.reshape(batch * sections, *value_cache.shape[3:]))
    here = tuple(pltpu.with_memory_space_constraint(value, pltpu.HBM) for value in here)
    there = tuple(other(value) for value in here)
    lens = mine(lengths)
    half = HD // 2
    frequency = 10000.0 ** (-(jnp.arange(half, dtype=jnp.float32) * 2.0) / HD)
    angles = lens.astype(jnp.float32)[:, None] * frequency[None, :]
    cosine, sine = jnp.cos(angles), jnp.sin(angles)
    cos = jnp.concatenate([cosine, cosine], axis=1)
    sin = jnp.concatenate([-sine, sine], axis=1)
    lens = jnp.broadcast_to(lens[:, None], (rows, HD))

    everyone = swap(jnp.broadcast_to(resid[None], (sections, batch, width)), "section")
    everyone, pre_gain, post_gain = lax.optimization_barrier((everyone, pre_gain, post_gain))
    gains = jnp.concatenate([pre_gain, post_gain], axis=0)
    other_gains = other(gains)
    by_layer = [jnp.where(core == 0, gains, other_gains), jnp.where(core == 0, other_gains, gains)]
    ids = jnp.arange(directions.shape[0], dtype=jnp.int32)
    one_hot = (mine(concept)[:, None] == ids[None, :]).astype(jnp.bfloat16)
    picked = jnp.dot(one_hot, directions, preferred_element_type=jnp.float32).astype(jnp.bfloat16)
    state = mine(everyone.reshape(batch * sections, width))
    both = jnp.concatenate(
        [jnp.broadcast_to(state[None], (lanes, rows, width)), picked.reshape(lanes, per, width)], axis=1
    )
    both = swap(both, "tensor")
    x = lax.dynamic_slice_in_dim(both, lane * per, per, 1).transpose(1, 0, 2).reshape(per, D)
    vectors = both[:, rows:].transpose(1, 0, 2).reshape(per, D).astype(jnp.float32)
    row = start + lane * per
    strengths = lax.dynamic_slice_in_dim(strength, row, per, 0)
    layers = lax.dynamic_slice_in_dim(steer_layer, row, per, 0)
    steers = [
        (strengths * (layers == 2 * plane + k).astype(jnp.float32))[:, None] * vectors for k in range(2)
    ]

    sels = [jnp.stack([jnp.where(core == k, 0, 1), core]).astype(jnp.int32) for k in range(2)]
    pre = [value[:1] for value in by_layer]
    post = [value[1:] for value in by_layer]
    cos, sin, lens, pre, post, steers, sels = lax.optimization_barrier(
        (cos, sin, lens, pre, post, steers, sels)
    )

    def gathered(x):
        return swap(jnp.broadcast_to(x[None], (lanes, per, D)), "tensor")

    share = batch // per
    source = section % planes * share
    x, both, source = lax.optimization_barrier((x, both, source))
    loaded = [None, None]
    for p in range(planes):
        if p:
            x = shifted(x, lambda s: (s + 2) % sections)
        for k in range(2):
            full = gathered(x) if p or k else both
            if p:
                parts = layer_call(full, per, pre[k], cos, sin, lens, loaded[k])
            else:
                parts, loaded[k] = opening_call(sels[k], full, per, pre[k], cos, sin, lens, here, there)
            x = combine_call(swap(parts, "tensor"), x, post[k], steers[k])
    pairs = [
        ((sections - 2 + c) * lanes + t, (c * planes + t // share) * lanes + t)
        for c in range(2)
        for t in range(lanes)
    ]
    x = lax.ppermute(x, ("section", "tensor"), pairs)
    pieces = swap(x.reshape(per, lanes, width).transpose(1, 0, 2), "tensor")
    out = lax.dynamic_slice_in_dim(pieces, source, share, 0)
    return out.reshape(batch, width)


def solution(mesh):
    placed = (
        P("section", "tensor"),
        P("section", None),
        P("section", None),
        P("section", None, "tensor"),
        P("section", None, "tensor"),
        P("section", None, "tensor"),
        P("section", "tensor", None),
        P("section", None, "tensor", None, None),
        P("section", None, "tensor", None, None),
        P(),
        P(),
        P(),
        P(),
        P(None, "tensor"),
    )
    return jax.shard_map(
        on_device, mesh=mesh, in_specs=placed, out_specs=P("section", "tensor"), check_vma=False
    )
```

```python
import jax
import jax.numpy as jnp
from jax import lax
from jax.experimental import pallas as pl
from jax.experimental.pallas import tpu as pltpu
from jax.sharding import PartitionSpec as P

D = 4608
HEADS = 32
KVH = 16
HD = 128
GROUP = HEADS // KVH
QW = GROUP * HD
CHUNKS = 6
DC = D // CHUNKS
EPS = 1e-06
CAP = 50.0
SCALE = float(D // HEADS) ** (-0.5)
SMEM = pl.BlockSpec(memory_space=pltpu.SMEM)
VMEM = pl.BlockSpec(memory_space=pltpu.VMEM)
ANY = pl.BlockSpec(memory_space=pl.ANY)


def turn(v, cos, sin):
    return v * cos + pltpu.roll(v, HD // 2, 1) * sin


def project(x_ref, pre_ref, cos_ref, sin_ref, len_ref, w, wo, kc, vc, o_ref, xs, ho, arrived):
    rows = xs.shape[0]
    ctx = kc.shape[1]
    blocks, per = o_ref.shape[0], o_ref.shape[1]
    if x_ref.shape[1] == per:
        for b in range(blocks):
            xs[pl.ds(b * per, per), :] = x_ref[b]
    else:
        width = x_ref.shape[2]
        for b in range(blocks):
            xs[:, pl.ds(b * width, width)] = x_ref[b, pl.ds(0, rows), :]
    acc = jnp.zeros((rows, QW + 2 * HD), jnp.float32)
    squares = jnp.zeros((rows, 1), jnp.float32)
    for c in range(CHUNKS):
        part = xs[:, pl.ds(c * DC, DC)].astype(jnp.float32)
        squares += jnp.sum(part * part, axis=1, keepdims=True)
        scaled = (part * pre_ref[:, pl.ds(c * DC, DC)]).astype(jnp.bfloat16)
        arrived(c)
        acc += jnp.dot(scaled, w[pl.ds(c * DC, DC), :], preferred_element_type=jnp.float32)
    acc = acc * lax.rsqrt(squares / D + EPS)
    cos, sin = cos_ref[...], sin_ref[...]
    heads = [turn(acc[:, h * HD:(h + 1) * HD], cos, sin).astype(jnp.bfloat16) for h in range(GROUP)]
    new_k = turn(acc[:, QW:QW + HD], cos, sin).astype(jnp.bfloat16).astype(jnp.float32)
    new_v = acc[:, QW + HD:].astype(jnp.bfloat16).astype(jnp.float32)
    arrived(CHUNKS)
    n = 8
    col = lax.broadcasted_iota(jnp.int32, (GROUP * n, n * ctx), 1)
    row = lax.broadcasted_iota(jnp.int32, (GROUP * n, n * ctx), 0)
    rel = col - (row % n) * ctx
    for g in range(rows // n):
        lo, hi = g * n, (g + 1) * n
        q = jnp.concatenate([h[lo:hi].astype(jnp.float32) for h in heads], axis=0)
        nk = jnp.concatenate([new_k[lo:hi]] * GROUP, axis=0)
        nv = jnp.concatenate([new_v[lo:hi]] * GROUP, axis=0)
        ln = jnp.concatenate([len_ref[lo:hi, :1]] * GROUP, axis=0)
        keys = kc[pl.ds(lo, n)].reshape(n * ctx, HD)
        vals = vc[pl.ds(lo, n)].reshape(n * ctx, HD)
        s = lax.dot_general(
            q.astype(jnp.bfloat16), keys, (((1,), (1,)), ((), ())), preferred_element_type=jnp.float32
        )
        own = jnp.sum(q * nk, axis=1, keepdims=True)
        wt = jnp.exp(CAP * jnp.tanh(s * (SCALE / CAP)) - CAP)
        wt = jnp.where((rel >= 0) & (rel < ln), wt, 0.0)
        own_w = jnp.exp(CAP * jnp.tanh(own * (SCALE / CAP)) - CAP)
        total = jnp.sum(wt, axis=1, keepdims=True) + own_w
        probs = (wt / total).astype(jnp.bfloat16)
        own_p = (own_w / total).astype(jnp.bfloat16).astype(jnp.float32)
        mixed = jnp.dot(probs, vals, preferred_element_type=jnp.float32) + own_p * nv
        for h in range(GROUP):
            ho[pl.ds(lo, n), pl.ds(h * HD, HD)] = mixed[h * n:(h + 1) * n]
    arrived(CHUNKS + 1)
    lhs = ho[...].astype(jnp.bfloat16)
    for c in range(CHUNKS):
        at = pl.ds(c * DC, DC)
        out = jnp.dot(lhs, wo[:, at], preferred_element_type=jnp.float32).astype(jnp.bfloat16)
        for b in range(blocks):
            o_ref[b, :, at] = out[b * per:(b + 1) * per]


def layer_kernel(on_ref, x_ref, pre_ref, cos_ref, sin_ref, len_ref, w, wo, kc, vc, o_ref, xs, ho):
    @pl.when(on_ref[0] != 0)
    def _():
        project(x_ref, pre_ref, cos_ref, sin_ref, len_ref, w, wo, kc, vc, o_ref, xs, ho, lambda step: None)


def opening_kernel(
    sel_ref, x_ref, pre_ref, cos_ref, sin_ref, len_ref,
    wq_a, wk_a, wv_a, wo_a, kc_a, vc_a,
    wq_b, wk_b, wv_b, wo_b, kc_b, vc_b,
    o_ref, w, wo, kc, vc,
    xs, ho, wsem, sem,
):
    rows = xs.shape[0]
    mine = pl.ds(pl.multiple_of(sel_ref[1] * rows, rows), rows)

    def copies(wq_hbm, wk_hbm, wv_hbm, wo_hbm, kc_hbm, vc_hbm):
        steps = []
        for c in range(CHUNKS):
            at = pl.ds(c * DC, DC)
            steps.append([
                pltpu.make_async_copy(wq_hbm.at[at], w.at[at, pl.ds(0, QW)], wsem.at[3 * c]),
                pltpu.make_async_copy(wk_hbm.at[at], w.at[at, pl.ds(QW, HD)], wsem.at[3 * c + 1]),
                pltpu.make_async_copy(wv_hbm.at[at], w.at[at, pl.ds(QW + HD, HD)], wsem.at[3 * c + 2]),
            ])
        steps.append([
            pltpu.make_async_copy(kc_hbm.at[mine], kc, sem.at[0]),
            pltpu.make_async_copy(vc_hbm.at[mine], vc, sem.at[1]),
        ])
        steps.append([pltpu.make_async_copy(wo_hbm, wo, sem.at[2])])
        return steps

    def begin(steps):
        for step in steps:
            for copy in step:
                copy.start()

    first = copies(wq_a, wk_a, wv_a, wo_a, kc_a, vc_a)

    @pl.when(sel_ref[0] == 0)
    def _():
        begin(first)

    @pl.when(sel_ref[0] != 0)
    def _():
        begin(copies(wq_b, wk_b, wv_b, wo_b, kc_b, vc_b))

    def arrived(step):
        for copy in first[step]:
            copy.wait()

    @pl.when(sel_ref[2] != 0)
    def _():
        project(x_ref, pre_ref, cos_ref, sin_ref, len_ref, w, wo, kc, vc, o_ref, xs, ho, arrived)

    @pl.when(sel_ref[2] == 0)
    def _():
        for step in range(len(first)):
            arrived(step)


def opening_call(sel, x, per, pre, cos, sin, lens, here, there):
    wo, kc, vc = here[3:]
    rows = lens.shape[0]
    shapes = [(rows // per, per, D), (D, QW + 2 * HD), wo.shape, (rows,) + kc.shape[1:], (rows,) + vc.shape[1:]]
    out, *loaded = pl.pallas_call(
        opening_kernel,
        out_shape=[jax.ShapeDtypeStruct(shape, jnp.bfloat16) for shape in shapes],
        in_specs=[SMEM] + [VMEM] * 5 + [ANY] * 12,
        out_specs=[VMEM] * 5,
        scratch_shapes=[
            pltpu.VMEM((rows, D), jnp.bfloat16),
            pltpu.VMEM((rows, QW), jnp.float32),
            pltpu.SemaphoreType.DMA((3 * CHUNKS,)),
            pltpu.SemaphoreType.DMA((3,)),
        ],
        compiler_params=pltpu.CompilerParams(vmem_limit_bytes=24 << 20),
        name="opening",
    )(sel, x, pre, cos, sin, lens, *here, *there)
    return out, loaded


def layer_call(on, x, per, pre, cos, sin, lens, loaded):
    rows = lens.shape[0]
    return pl.pallas_call(
        layer_kernel,
        out_shape=jax.ShapeDtypeStruct((rows // per, per, D), jnp.bfloat16),
        in_specs=[SMEM] + [VMEM] * 9,
        out_specs=VMEM,
        scratch_shapes=[pltpu.VMEM((rows, D), jnp.bfloat16), pltpu.VMEM((rows, QW), jnp.float32)],
        compiler_params=pltpu.CompilerParams(vmem_limit_bytes=14 << 20),
        name="layer",
    )(on, x, pre, cos, sin, lens, *loaded)


def combine_kernel(p_ref, x_ref, post_ref, steer_ref, o_ref):
    total = p_ref[0].astype(jnp.float32)
    for b in range(1, p_ref.shape[0]):
        total += p_ref[b].astype(jnp.float32)
    factor = lax.rsqrt(jnp.mean(total * total, axis=1, keepdims=True) + EPS)
    post = total * factor * post_ref[...]
    o_ref[...] = (x_ref[...].astype(jnp.float32) + post + steer_ref[...]).astype(jnp.bfloat16)


def combine_call(parts, x, post, steer):
    return pl.pallas_call(
        combine_kernel,
        out_shape=jax.ShapeDtypeStruct(x.shape, jnp.bfloat16),
        in_specs=[VMEM] * 4,
        out_specs=VMEM,
        compiler_params=pltpu.CompilerParams(vmem_limit_bytes=8 << 20),
        name="combine",
    )(parts, x, post, steer)


def cut_kernel(x_ref, o_ref):
    width = o_ref.shape[2]
    for t in range(o_ref.shape[0]):
        o_ref[t] = x_ref[:, pl.ds(t * width, width)]


def cut_call(x, lanes):
    rows, width = x.shape
    return pl.pallas_call(
        cut_kernel,
        out_shape=jax.ShapeDtypeStruct((lanes, rows, width // lanes), x.dtype),
        in_specs=[VMEM],
        out_specs=VMEM,
        compiler_params=pltpu.CompilerParams(vmem_limit_bytes=4 << 20),
        name="cut",
    )(x)


def merge_kernel(from_ref, p_ref, o_ref):
    per = p_ref.shape[1]
    for k in range(o_ref.shape[0] // per):
        o_ref[pl.ds(k * per, per), :] = p_ref[from_ref[0] + k]


def merge_call(source, pieces, rows):
    return pl.pallas_call(
        merge_kernel,
        out_shape=jax.ShapeDtypeStruct((rows, pieces.shape[2]), pieces.dtype),
        in_specs=[SMEM, VMEM],
        out_specs=VMEM,
        compiler_params=pltpu.CompilerParams(vmem_limit_bytes=4 << 20),
        name="merge",
    )(source, pieces)


def swap(value, axis):
    return lax.all_to_all(value, axis, 0, 0, tiled=True)


def on_device(
    resid, pre_gain, post_gain, w_query, w_key, w_value, w_out, key_cache, value_cache,
    lengths, concept, steer_layer, strength, directions,
):
    sections = lax.axis_size("section")
    lanes = lax.axis_size("tensor")
    section = lax.axis_index("section")
    lane = lax.axis_index("tensor")
    batch, width = resid.shape
    planes, core, plane = sections // 2, section % 2, section // 2
    rows = batch * planes
    per = rows // lanes
    start = core * rows

    def shifted(value, target):
        pairs = [(s * lanes + t, target(s) * lanes + t) for s in range(sections) for t in range(lanes)]
        return lax.ppermute(value, ("section", "tensor"), pairs)

    def other(value):
        return shifted(value, lambda s: s ^ 1)

    def mine(value):
        return lax.dynamic_slice_in_dim(value, start, rows, 0)

    here = (w_query[0], w_key[0], w_value[0], w_out[0],
            key_cache.reshape(batch * sections, *key_cache.shape[3:]),
            value_cache.reshape(batch * sections, *value_cache.shape[3:]))
    here = tuple(pltpu.with_memory_space_constraint(value, pltpu.HBM) for value in here)
    there = tuple(other(value) for value in here)
    lens = mine(lengths)
    half = HD // 2
    frequency = 10000.0 ** (-(jnp.arange(half, dtype=jnp.float32) * 2.0) / HD)
    angles = lens.astype(jnp.float32)[:, None] * frequency[None, :]
    cosine, sine = jnp.cos(angles), jnp.sin(angles)
    cos = jnp.concatenate([cosine, cosine], axis=1)
    sin = jnp.concatenate([-sine, sine], axis=1)
    lens = jnp.broadcast_to(lens[:, None], (rows, HD))

    everyone = swap(jnp.broadcast_to(resid[None], (sections, batch, width)), "section")
    pre, post = [
        [jnp.where(core == 0, own, far), jnp.where(core == 0, far, own)]
        for own, far in ((pre_gain, other(pre_gain)), (post_gain, other(post_gain)))
    ]
    ids = jnp.arange(directions.shape[0], dtype=jnp.int32)
    one_hot = (mine(concept)[:, None] == ids[None, :]).astype(jnp.bfloat16)
    picked = jnp.dot(one_hot, directions, preferred_element_type=jnp.float32).astype(jnp.bfloat16)
    state = mine(everyone.reshape(batch * sections, width))
    both = jnp.concatenate(
        [jnp.broadcast_to(state[None], (lanes, rows, width)), picked.reshape(lanes, per, width)], axis=1
    )
    both = swap(both, "tensor")
    x = lax.dynamic_slice_in_dim(both, lane * per, per, 1).transpose(1, 0, 2).reshape(per, D)
    vectors = both[:, rows:].transpose(1, 0, 2).reshape(per, D).astype(jnp.float32)
    row = start + lane * per
    strengths = lax.dynamic_slice_in_dim(strength, row, per, 0)
    layers = lax.dynamic_slice_in_dim(steer_layer, row, per, 0)
    steers = [
        (strengths * (layers == 2 * plane + k).astype(jnp.float32))[:, None] * vectors for k in range(2)
    ]

    sels = [
        jnp.stack([jnp.where(core == k, 0, 1), core, (plane == 0).astype(jnp.int32)]).astype(jnp.int32)
        for k in range(2)
    ]
    turns = [(plane == p).astype(jnp.int32).reshape(1) for p in range(planes)]
    cos, sin, lens, pre, post, steers, sels = lax.optimization_barrier(
        (cos, sin, lens, pre, post, steers, sels)
    )

    def gathered(x):
        return swap(jnp.broadcast_to(x[None], (lanes, per, D)), "tensor")

    share = batch // per
    source = section % planes * share
    source = source.astype(jnp.int32).reshape(1)
    x, both, source, turns = lax.optimization_barrier((x, both, source, turns))
    loaded = [None, None]
    for p in range(planes):
        if p:
            x = shifted(x, lambda s: (s + 2) % sections)
        for k in range(2):
            full = gathered(x) if p or k else both
            if p:
                parts = layer_call(turns[p], full, per, pre[k], cos, sin, lens, loaded[k])
            else:
                parts, loaded[k] = opening_call(sels[k], full, per, pre[k], cos, sin, lens, here, there)
            x = combine_call(swap(parts, "tensor"), x, post[k], steers[k])
    pairs = [
        ((sections - 2 + c) * lanes + t, (c * planes + t // share) * lanes + t)
        for c in range(2)
        for t in range(lanes)
    ]
    x = lax.ppermute(x, ("section", "tensor"), pairs)
    return merge_call(source, swap(cut_call(x, lanes), "tensor"), batch)


def solution(mesh):
    placed = (
        P("section", "tensor"),
        P("section", None),
        P("section", None),
        P("section", None, "tensor"),
        P("section", None, "tensor"),
        P("section", None, "tensor"),
        P("section", "tensor", None),
        P("section", None, "tensor", None, None),
        P("section", None, "tensor", None, None),
        P(),
        P(),
        P(),
        P(),
        P(None, "tensor"),
    )
    return jax.shard_map(
        on_device, mesh=mesh, in_specs=placed, out_specs=P("section", "tensor"), check_vma=False
    )
```

```python
import jax
import jax.numpy as jnp
from jax import lax
from jax.experimental import pallas as pl
from jax.experimental.pallas import tpu as pltpu
from jax.sharding import PartitionSpec as P

D = 4608
HEADS = 32
KVH = 16
HD = 128
GROUP = HEADS // KVH
QW = GROUP * HD
CHUNKS = 6
DC = D // CHUNKS
EPS = 1e-06
CAP = 50.0
SCALE = float(D // HEADS) ** (-0.5)
SMEM = pl.BlockSpec(memory_space=pltpu.SMEM)
VMEM = pl.BlockSpec(memory_space=pltpu.VMEM)
ANY = pl.BlockSpec(memory_space=pl.ANY)


def turn(v, cos, sin):
    return v * cos + pltpu.roll(v, HD // 2, 1) * sin


def project(x_ref, pre_ref, cos_ref, sin_ref, len_ref, w, wo, kc, vc, o_ref, xs, ho, arrived):
    rows = xs.shape[0]
    ctx = kc.shape[1]
    blocks, per = o_ref.shape[0], o_ref.shape[1]
    if x_ref.shape[1] == per:
        for b in range(blocks):
            xs[pl.ds(b * per, per), :] = x_ref[b]
    else:
        width = x_ref.shape[2]
        for b in range(blocks):
            xs[:, pl.ds(b * width, width)] = x_ref[b, pl.ds(0, rows), :]
    acc = jnp.zeros((rows, QW + 2 * HD), jnp.float32)
    squares = jnp.zeros((rows, 1), jnp.float32)
    for c in range(CHUNKS):
        part = xs[:, pl.ds(c * DC, DC)].astype(jnp.float32)
        squares += jnp.sum(part * part, axis=1, keepdims=True)
        scaled = (part * pre_ref[:, pl.ds(c * DC, DC)]).astype(jnp.bfloat16)
        arrived(c)
        acc += jnp.dot(scaled, w[pl.ds(c * DC, DC), :], preferred_element_type=jnp.float32)
    acc = acc * lax.rsqrt(squares / D + EPS)
    cos, sin = cos_ref[...], sin_ref[...]
    heads = [turn(acc[:, h * HD:(h + 1) * HD], cos, sin).astype(jnp.bfloat16) for h in range(GROUP)]
    new_k = turn(acc[:, QW:QW + HD], cos, sin).astype(jnp.bfloat16).astype(jnp.float32)
    new_v = acc[:, QW + HD:].astype(jnp.bfloat16).astype(jnp.float32)
    arrived(CHUNKS)
    n = 8
    col = lax.broadcasted_iota(jnp.int32, (GROUP * n, n * ctx), 1)
    row = lax.broadcasted_iota(jnp.int32, (GROUP * n, n * ctx), 0)
    rel = col - (row % n) * ctx
    for g in range(rows // n):
        lo, hi = g * n, (g + 1) * n
        q = jnp.concatenate([h[lo:hi].astype(jnp.float32) for h in heads], axis=0)
        nk = jnp.concatenate([new_k[lo:hi]] * GROUP, axis=0)
        nv = jnp.concatenate([new_v[lo:hi]] * GROUP, axis=0)
        ln = jnp.concatenate([len_ref[lo:hi, :1]] * GROUP, axis=0)
        keys = kc[pl.ds(lo, n)].reshape(n * ctx, HD)
        vals = vc[pl.ds(lo, n)].reshape(n * ctx, HD)
        s = lax.dot_general(
            q.astype(jnp.bfloat16), keys, (((1,), (1,)), ((), ())), preferred_element_type=jnp.float32
        )
        own = jnp.sum(q * nk, axis=1, keepdims=True)
        wt = jnp.exp(CAP * jnp.tanh(s * (SCALE / CAP)) - CAP)
        wt = jnp.where((rel >= 0) & (rel < ln), wt, 0.0)
        own_w = jnp.exp(CAP * jnp.tanh(own * (SCALE / CAP)) - CAP)
        total = jnp.sum(wt, axis=1, keepdims=True) + own_w
        probs = (wt / total).astype(jnp.bfloat16)
        own_p = (own_w / total).astype(jnp.bfloat16).astype(jnp.float32)
        mixed = jnp.dot(probs, vals, preferred_element_type=jnp.float32) + own_p * nv
        for h in range(GROUP):
            ho[pl.ds(lo, n), pl.ds(h * HD, HD)] = mixed[h * n:(h + 1) * n]
    arrived(CHUNKS + 1)
    lhs = ho[...].astype(jnp.bfloat16)
    for c in range(CHUNKS):
        at = pl.ds(c * DC, DC)
        out = jnp.dot(lhs, wo[:, at], preferred_element_type=jnp.float32).astype(jnp.bfloat16)
        for b in range(blocks):
            o_ref[b, :, at] = out[b * per:(b + 1) * per]


def layer_kernel(on_ref, x_ref, pre_ref, cos_ref, sin_ref, len_ref, w, wo, kc, vc, o_ref, xs, ho):
    @pl.when(on_ref[0] != 0)
    def _():
        project(x_ref, pre_ref, cos_ref, sin_ref, len_ref, w, wo, kc, vc, o_ref, xs, ho, lambda step: None)


def opening_kernel(
    sel_ref, x_ref, pre_ref, cos_ref, sin_ref, len_ref,
    wq_a, wk_a, wv_a, wo_a, kc_a, vc_a,
    wq_b, wk_b, wv_b, wo_b, kc_b, vc_b,
    o_ref, w0, wo0, kc0, vc0, w1, wo1, kc1, vc1,
    xs, ho, wsem, sem, late_sem,
):
    rows = xs.shape[0]
    mine = pl.ds(pl.multiple_of(sel_ref[0] * rows, rows), rows)
    here = (wq_a, wk_a, wv_a, wo_a, kc_a, vc_a)
    there = (wq_b, wk_b, wv_b, wo_b, kc_b, vc_b)

    def pieces(source, w, at):
        return (
            (source[0].at[at], w.at[at, pl.ds(0, QW)]),
            (source[1].at[at], w.at[at, pl.ds(QW, HD)]),
            (source[2].at[at], w.at[at, pl.ds(QW + HD, HD)]),
        )

    def early(source):
        steps = []
        for c in range(CHUNKS):
            at = pl.ds(c * DC, DC)
            steps.append([
                pltpu.make_async_copy(src, dst, wsem.at[3 * c + i])
                for i, (src, dst) in enumerate(pieces(source, w0, at))
            ])
        steps.append([
            pltpu.make_async_copy(source[4].at[mine], kc0, sem.at[0]),
            pltpu.make_async_copy(source[5].at[mine], vc0, sem.at[1]),
        ])
        steps.append([pltpu.make_async_copy(source[3], wo0, sem.at[2])])
        return steps

    def late(source):
        copies = [
            pltpu.make_async_copy(src, dst, late_sem.at[i])
            for i, (src, dst) in enumerate(pieces(source, w1, pl.ds(0, D)))
        ]
        return copies + [
            pltpu.make_async_copy(source[4].at[mine], kc1, late_sem.at[3]),
            pltpu.make_async_copy(source[5].at[mine], vc1, late_sem.at[4]),
            pltpu.make_async_copy(source[3], wo1, late_sem.at[5]),
        ]

    first, second = early(here), late(there)

    def begin_early(steps):
        for step in steps:
            for copy in step:
                copy.start()

    @pl.when(sel_ref[0] == 0)
    def _():
        begin_early(first)

    @pl.when(sel_ref[0] != 0)
    def _():
        begin_early(early(there))

    def begin_late():
        @pl.when(sel_ref[0] == 0)
        def _():
            for copy in second:
                copy.start()

        @pl.when(sel_ref[0] != 0)
        def _():
            for copy in late(here):
                copy.start()

    def arrived(step):
        for copy in first[step]:
            copy.wait()
        if step == CHUNKS - 1:
            begin_late()

    @pl.when(sel_ref[1] != 0)
    def _():
        project(x_ref, pre_ref, cos_ref, sin_ref, len_ref, w0, wo0, kc0, vc0, o_ref, xs, ho, arrived)

    @pl.when(sel_ref[1] == 0)
    def _():
        for step in range(len(first)):
            arrived(step)

    for copy in second:
        copy.wait()


def opening_call(sel, x, per, pre, cos, sin, lens, here, there):
    wo, kc, vc = here[3:]
    rows = lens.shape[0]
    kept = [(D, QW + 2 * HD), wo.shape, (rows,) + kc.shape[1:], (rows,) + vc.shape[1:]]
    shapes = [(rows // per, per, D)] + kept + kept
    out, *loaded = pl.pallas_call(
        opening_kernel,
        out_shape=[jax.ShapeDtypeStruct(shape, jnp.bfloat16) for shape in shapes],
        in_specs=[SMEM] + [VMEM] * 5 + [ANY] * 12,
        out_specs=[VMEM] * 9,
        scratch_shapes=[
            pltpu.VMEM((rows, D), jnp.bfloat16),
            pltpu.VMEM((rows, QW), jnp.float32),
            pltpu.SemaphoreType.DMA((3 * CHUNKS,)),
            pltpu.SemaphoreType.DMA((3,)),
            pltpu.SemaphoreType.DMA((6,)),
        ],
        compiler_params=pltpu.CompilerParams(vmem_limit_bytes=28 << 20),
        name="opening",
    )(sel, x, pre, cos, sin, lens, *here, *there)
    return out, loaded[:4], loaded[4:]


def layer_call(on, x, per, pre, cos, sin, lens, loaded):
    rows = lens.shape[0]
    return pl.pallas_call(
        layer_kernel,
        out_shape=jax.ShapeDtypeStruct((rows // per, per, D), jnp.bfloat16),
        in_specs=[SMEM] + [VMEM] * 9,
        out_specs=VMEM,
        scratch_shapes=[pltpu.VMEM((rows, D), jnp.bfloat16), pltpu.VMEM((rows, QW), jnp.float32)],
        compiler_params=pltpu.CompilerParams(vmem_limit_bytes=14 << 20),
        name="layer",
    )(on, x, pre, cos, sin, lens, *loaded)


def combine_kernel(p_ref, x_ref, post_ref, steer_ref, o_ref, *copies_ref):
    total = p_ref[0].astype(jnp.float32)
    for b in range(1, p_ref.shape[0]):
        total += p_ref[b].astype(jnp.float32)
    factor = lax.rsqrt(jnp.mean(total * total, axis=1, keepdims=True) + EPS)
    post = total * factor * post_ref[...]
    out = (x_ref[...].astype(jnp.float32) + post + steer_ref[...]).astype(jnp.bfloat16)
    o_ref[...] = out
    for ref in copies_ref:
        for b in range(ref.shape[0]):
            ref[b] = out


def combine_call(parts, x, post, steer, copies):
    shapes = [x.shape] + ([(copies,) + x.shape] if copies else [])
    return pl.pallas_call(
        combine_kernel,
        out_shape=[jax.ShapeDtypeStruct(shape, x.dtype) for shape in shapes],
        in_specs=[VMEM] * 4,
        out_specs=[VMEM] * len(shapes),
        compiler_params=pltpu.CompilerParams(vmem_limit_bytes=8 << 20),
        name="combine",
    )(parts, x, post, steer)


def cut_kernel(x_ref, o_ref):
    width = o_ref.shape[2]
    for t in range(o_ref.shape[0]):
        o_ref[t] = x_ref[:, pl.ds(t * width, width)]


def cut_call(x, lanes):
    rows, width = x.shape
    return pl.pallas_call(
        cut_kernel,
        out_shape=jax.ShapeDtypeStruct((lanes, rows, width // lanes), x.dtype),
        in_specs=[VMEM],
        out_specs=VMEM,
        compiler_params=pltpu.CompilerParams(vmem_limit_bytes=4 << 20),
        name="cut",
    )(x)


def merge_kernel(from_ref, p_ref, o_ref):
    per = p_ref.shape[1]
    for k in range(o_ref.shape[0] // per):
        o_ref[pl.ds(k * per, per), :] = p_ref[from_ref[0] + k]


def merge_call(source, pieces, rows):
    return pl.pallas_call(
        merge_kernel,
        out_shape=jax.ShapeDtypeStruct((rows, pieces.shape[2]), pieces.dtype),
        in_specs=[SMEM, VMEM],
        out_specs=VMEM,
        compiler_params=pltpu.CompilerParams(vmem_limit_bytes=4 << 20),
        name="merge",
    )(source, pieces)


def swap(value, axis):
    return lax.all_to_all(value, axis, 0, 0, tiled=True)


def on_device(
    resid, pre_gain, post_gain, w_query, w_key, w_value, w_out, key_cache, value_cache,
    lengths, concept, steer_layer, strength, directions,
):
    sections = lax.axis_size("section")
    lanes = lax.axis_size("tensor")
    section = lax.axis_index("section")
    lane = lax.axis_index("tensor")
    batch, width = resid.shape
    planes, core, plane = sections // 2, section % 2, section // 2
    rows = batch * planes
    per = rows // lanes
    start = core * rows

    def shifted(value, target):
        pairs = [(s * lanes + t, target(s) * lanes + t) for s in range(sections) for t in range(lanes)]
        return lax.ppermute(value, ("section", "tensor"), pairs)

    def other(value):
        return shifted(value, lambda s: s ^ 1)

    def mine(value):
        return lax.dynamic_slice_in_dim(value, start, rows, 0)

    here = (w_query[0], w_key[0], w_value[0], w_out[0],
            key_cache.reshape(batch * sections, *key_cache.shape[3:]),
            value_cache.reshape(batch * sections, *value_cache.shape[3:]))
    here = tuple(pltpu.with_memory_space_constraint(value, pltpu.HBM) for value in here)
    there = tuple(other(value) for value in here)
    lens = mine(lengths)
    half = HD // 2
    frequency = 10000.0 ** (-(jnp.arange(half, dtype=jnp.float32) * 2.0) / HD)
    angles = lens.astype(jnp.float32)[:, None] * frequency[None, :]
    cosine, sine = jnp.cos(angles), jnp.sin(angles)
    cos = jnp.concatenate([cosine, cosine], axis=1)
    sin = jnp.concatenate([-sine, sine], axis=1)
    lens = jnp.broadcast_to(lens[:, None], (rows, HD))

    everyone = swap(jnp.broadcast_to(resid[None], (sections, batch, width)), "section")
    pre, post = [
        [jnp.where(core == 0, own, far), jnp.where(core == 0, far, own)]
        for own, far in ((pre_gain, other(pre_gain)), (post_gain, other(post_gain)))
    ]
    ids = jnp.arange(directions.shape[0], dtype=jnp.int32)
    one_hot = (mine(concept)[:, None] == ids[None, :]).astype(jnp.bfloat16)
    picked = jnp.dot(one_hot, directions, preferred_element_type=jnp.float32).astype(jnp.bfloat16)
    state = mine(everyone.reshape(batch * sections, width))
    both = jnp.concatenate(
        [jnp.broadcast_to(state[None], (lanes, rows, width)), picked.reshape(lanes, per, width)], axis=1
    )
    both = swap(both, "tensor")
    x = lax.dynamic_slice_in_dim(both, lane * per, per, 1).transpose(1, 0, 2).reshape(per, D)
    vectors = both[:, rows:].transpose(1, 0, 2).reshape(per, D).astype(jnp.float32)
    row = start + lane * per
    strengths = lax.dynamic_slice_in_dim(strength, row, per, 0)
    layers = lax.dynamic_slice_in_dim(steer_layer, row, per, 0)
    steers = [
        (strengths * (layers == 2 * plane + k).astype(jnp.float32))[:, None] * vectors for k in range(2)
    ]

    sels = jnp.stack([core, (plane == 0).astype(jnp.int32)]).astype(jnp.int32)
    turns = [(plane == p).astype(jnp.int32).reshape(1) for p in range(planes)]
    cos, sin, lens, pre, post, steers, sels = lax.optimization_barrier(
        (cos, sin, lens, pre, post, steers, sels)
    )

    def gathered(x):
        return swap(jnp.broadcast_to(x[None], (lanes, per, D)), "tensor")

    share = batch // per
    source = section % planes * share
    source = source.astype(jnp.int32).reshape(1)
    x, both, source, turns = lax.optimization_barrier((x, both, source, turns))
    full = both
    for p in range(planes):
        if p:
            x = shifted(x, lambda s: (s + 2) % sections)
            full = gathered(x)
        if p:
            parts = layer_call(turns[p], full, per, pre[0], cos, sin, lens, loaded[0])
        else:
            parts, *loaded = opening_call(sels, full, per, pre[0], cos, sin, lens, here, there)
        x, copies = combine_call(swap(parts, "tensor"), x, post[0], steers[0], lanes)
        parts = layer_call(turns[p], swap(copies, "tensor"), per, pre[1], cos, sin, lens, loaded[1])
        x, = combine_call(swap(parts, "tensor"), x, post[1], steers[1], 0)
    pairs = [
        ((sections - 2 + c) * lanes + t, (c * planes + t // share) * lanes + t)
        for c in range(2)
        for t in range(lanes)
    ]
    x = lax.ppermute(x, ("section", "tensor"), pairs)
    return merge_call(source, swap(cut_call(x, lanes), "tensor"), batch)


def solution(mesh):
    placed = (
        P("section", "tensor"),
        P("section", None),
        P("section", None),
        P("section", None, "tensor"),
        P("section", None, "tensor"),
        P("section", None, "tensor"),
        P("section", "tensor", None),
        P("section", None, "tensor", None, None),
        P("section", None, "tensor", None, None),
        P(),
        P(),
        P(),
        P(),
        P(None, "tensor"),
    )
    return jax.shard_map(
        on_device, mesh=mesh, in_specs=placed, out_specs=P("section", "tensor"), check_vma=False
    )
```

```python
import jax
import jax.numpy as jnp
from jax import lax
from jax.experimental import pallas as pl
from jax.experimental.pallas import tpu as pltpu
from jax.sharding import PartitionSpec as P

D = 4608
HEADS = 32
KVH = 16
HD = 128
GROUP = HEADS // KVH
QW = GROUP * HD
CHUNKS = 6
DC = D // CHUNKS
EPS = 1e-06
CAP = 50.0
SCALE = float(D // HEADS) ** (-0.5)
SMEM = pl.BlockSpec(memory_space=pltpu.SMEM)
VMEM = pl.BlockSpec(memory_space=pltpu.VMEM)
ANY = pl.BlockSpec(memory_space=pl.ANY)


def turn(v, cos, sin):
    return v * cos + pltpu.roll(v, HD // 2, 1) * sin


def project(x_ref, pre_ref, cos_ref, sin_ref, len_ref, w, wo, kc, vc, o_ref, xs, ho, arrived):
    rows = xs.shape[0]
    ctx = kc.shape[1]
    blocks, per = o_ref.shape[0], o_ref.shape[1]
    if x_ref.shape[1] == per:
        for b in range(blocks):
            xs[pl.ds(b * per, per), :] = x_ref[b]
    else:
        width = x_ref.shape[2]
        for b in range(blocks):
            xs[:, pl.ds(b * width, width)] = x_ref[b, pl.ds(0, rows), :]
    acc = jnp.zeros((rows, QW + 2 * HD), jnp.float32)
    squares = jnp.zeros((rows, 1), jnp.float32)
    for c in range(CHUNKS):
        part = xs[:, pl.ds(c * DC, DC)].astype(jnp.float32)
        squares += jnp.sum(part * part, axis=1, keepdims=True)
        scaled = (part * pre_ref[:, pl.ds(c * DC, DC)]).astype(jnp.bfloat16)
        arrived(c)
        acc += jnp.dot(scaled, w[pl.ds(c * DC, DC), :], preferred_element_type=jnp.float32)
    acc = acc * lax.rsqrt(squares / D + EPS)
    cos, sin = cos_ref[...], sin_ref[...]
    heads = [turn(acc[:, h * HD:(h + 1) * HD], cos, sin).astype(jnp.bfloat16) for h in range(GROUP)]
    new_k = turn(acc[:, QW:QW + HD], cos, sin).astype(jnp.bfloat16).astype(jnp.float32)
    new_v = acc[:, QW + HD:].astype(jnp.bfloat16).astype(jnp.float32)
    arrived(CHUNKS)
    n = rows
    col = lax.broadcasted_iota(jnp.int32, (GROUP * n, n * ctx), 1)
    row = lax.broadcasted_iota(jnp.int32, (GROUP * n, n * ctx), 0)
    rel = col - (row % n) * ctx
    rel = jnp.where(rel < 0, n * ctx, rel)
    for g in range(rows // n):
        lo, hi = g * n, (g + 1) * n
        q = jnp.concatenate([h[lo:hi].astype(jnp.float32) for h in heads], axis=0)
        nk = jnp.concatenate([new_k[lo:hi]] * GROUP, axis=0)
        nv = jnp.concatenate([new_v[lo:hi]] * GROUP, axis=0)
        ln = jnp.concatenate([len_ref[lo:hi, :1]] * GROUP, axis=0)
        keys = kc[pl.ds(lo, n)].reshape(n * ctx, HD)
        vals = vc[pl.ds(lo, n)].reshape(n * ctx, HD)
        s = lax.dot_general(
            q.astype(jnp.bfloat16), keys, (((1,), (1,)), ((), ())), preferred_element_type=jnp.float32
        )
        own = jnp.sum(q * nk, axis=1, keepdims=True)
        wt = jnp.exp(CAP * jnp.tanh(s * (SCALE / CAP)) - CAP)
        wt = jnp.where(rel < ln, wt, 0.0)
        own_w = jnp.exp(CAP * jnp.tanh(own * (SCALE / CAP)) - CAP)
        total = jnp.sum(wt, axis=1, keepdims=True) + own_w
        probs = (wt / total).astype(jnp.bfloat16)
        own_p = (own_w / total).astype(jnp.bfloat16).astype(jnp.float32)
        mixed = jnp.dot(probs, vals, preferred_element_type=jnp.float32) + own_p * nv
        for h in range(GROUP):
            ho[pl.ds(lo, n), pl.ds(h * HD, HD)] = mixed[h * n:(h + 1) * n]
    arrived(CHUNKS + 1)
    lhs = ho[...].astype(jnp.bfloat16)
    for c in range(CHUNKS):
        at = pl.ds(c * DC, DC)
        out = jnp.dot(lhs, wo[:, at], preferred_element_type=jnp.float32).astype(jnp.bfloat16)
        for b in range(blocks):
            o_ref[b, :, at] = out[b * per:(b + 1) * per]


def layer_kernel(on_ref, x_ref, pre_ref, cos_ref, sin_ref, len_ref, w, wo, kc, vc, o_ref, xs, ho):
    @pl.when(on_ref[0] != 0)
    def _():
        project(x_ref, pre_ref, cos_ref, sin_ref, len_ref, w, wo, kc, vc, o_ref, xs, ho, lambda step: None)


def opening_kernel(
    sel_ref, x_ref, pre_ref, cos_ref, sin_ref, len_ref,
    wq_a, wk_a, wv_a, wo_a, kc_a, vc_a,
    wq_b, wk_b, wv_b, wo_b, kc_b, vc_b,
    o_ref, w0, wo0, kc0, vc0, w1, wo1, kc1, vc1,
    xs, ho, wsem, sem, late_sem,
):
    rows = xs.shape[0]
    mine = pl.ds(pl.multiple_of(sel_ref[0] * rows, rows), rows)
    here = (wq_a, wk_a, wv_a, wo_a, kc_a, vc_a)
    there = (wq_b, wk_b, wv_b, wo_b, kc_b, vc_b)

    def pieces(source, w, at):
        return (
            (source[0].at[at], w.at[at, pl.ds(0, QW)]),
            (source[1].at[at], w.at[at, pl.ds(QW, HD)]),
            (source[2].at[at], w.at[at, pl.ds(QW + HD, HD)]),
        )

    def early(source):
        steps = []
        for c in range(CHUNKS):
            at = pl.ds(c * DC, DC)
            steps.append([
                pltpu.make_async_copy(src, dst, wsem.at[3 * c + i])
                for i, (src, dst) in enumerate(pieces(source, w0, at))
            ])
        steps.append([
            pltpu.make_async_copy(source[4].at[mine], kc0, sem.at[0]),
            pltpu.make_async_copy(source[5].at[mine], vc0, sem.at[1]),
        ])
        steps.append([pltpu.make_async_copy(source[3], wo0, sem.at[2])])
        return steps

    def late(source):
        copies = [
            pltpu.make_async_copy(src, dst, late_sem.at[i])
            for i, (src, dst) in enumerate(pieces(source, w1, pl.ds(0, D)))
        ]
        return copies + [
            pltpu.make_async_copy(source[4].at[mine], kc1, late_sem.at[3]),
            pltpu.make_async_copy(source[5].at[mine], vc1, late_sem.at[4]),
            pltpu.make_async_copy(source[3], wo1, late_sem.at[5]),
        ]

    first, second = early(here), late(there)

    def begin_early(steps):
        for step in steps:
            for copy in step:
                copy.start()

    @pl.when(sel_ref[0] == 0)
    def _():
        begin_early(first)

    @pl.when(sel_ref[0] != 0)
    def _():
        begin_early(early(there))

    def begin_late():
        @pl.when(sel_ref[0] == 0)
        def _():
            for copy in second:
                copy.start()

        @pl.when(sel_ref[0] != 0)
        def _():
            for copy in late(here):
                copy.start()

    def arrived(step):
        for copy in first[step]:
            copy.wait()
        if step == CHUNKS - 1:
            begin_late()

    @pl.when(sel_ref[1] != 0)
    def _():
        project(x_ref, pre_ref, cos_ref, sin_ref, len_ref, w0, wo0, kc0, vc0, o_ref, xs, ho, arrived)

    @pl.when(sel_ref[1] == 0)
    def _():
        for step in range(len(first)):
            arrived(step)

    for copy in second:
        copy.wait()


def opening_call(sel, x, per, pre, cos, sin, lens, here, there):
    wo, kc, vc = here[3:]
    rows = lens.shape[0]
    kept = [(D, QW + 2 * HD), wo.shape, (rows,) + kc.shape[1:], (rows,) + vc.shape[1:]]
    shapes = [(rows // per, per, D)] + kept + kept
    out, *loaded = pl.pallas_call(
        opening_kernel,
        out_shape=[jax.ShapeDtypeStruct(shape, jnp.bfloat16) for shape in shapes],
        in_specs=[SMEM] + [VMEM] * 5 + [ANY] * 12,
        out_specs=[VMEM] * 9,
        scratch_shapes=[
            pltpu.VMEM((rows, D), jnp.bfloat16),
            pltpu.VMEM((rows, QW), jnp.float32),
            pltpu.SemaphoreType.DMA((3 * CHUNKS,)),
            pltpu.SemaphoreType.DMA((3,)),
            pltpu.SemaphoreType.DMA((6,)),
        ],
        compiler_params=pltpu.CompilerParams(vmem_limit_bytes=28 << 20),
        name="opening",
    )(sel, x, pre, cos, sin, lens, *here, *there)
    return out, loaded[:4], loaded[4:]


def layer_call(on, x, per, pre, cos, sin, lens, loaded):
    rows = lens.shape[0]
    return pl.pallas_call(
        layer_kernel,
        out_shape=jax.ShapeDtypeStruct((rows // per, per, D), jnp.bfloat16),
        in_specs=[SMEM] + [VMEM] * 9,
        out_specs=VMEM,
        scratch_shapes=[pltpu.VMEM((rows, D), jnp.bfloat16), pltpu.VMEM((rows, QW), jnp.float32)],
        compiler_params=pltpu.CompilerParams(vmem_limit_bytes=14 << 20),
        name="layer",
    )(on, x, pre, cos, sin, lens, *loaded)


def combine_kernel(p_ref, x_ref, post_ref, steer_ref, o_ref, *copies_ref):
    total = p_ref[0].astype(jnp.float32)
    for b in range(1, p_ref.shape[0]):
        total += p_ref[b].astype(jnp.float32)
    factor = lax.rsqrt(jnp.mean(total * total, axis=1, keepdims=True) + EPS)
    post = total * factor * post_ref[...]
    out = (x_ref[...].astype(jnp.float32) + post + steer_ref[...]).astype(jnp.bfloat16)
    o_ref[...] = out
    for ref in copies_ref:
        for b in range(ref.shape[0]):
            ref[b] = out


def combine_call(parts, x, post, steer, copies):
    shapes = [x.shape] + ([(copies,) + x.shape] if copies else [])
    return pl.pallas_call(
        combine_kernel,
        out_shape=[jax.ShapeDtypeStruct(shape, x.dtype) for shape in shapes],
        in_specs=[VMEM] * 4,
        out_specs=[VMEM] * len(shapes),
        compiler_params=pltpu.CompilerParams(vmem_limit_bytes=8 << 20),
        name="combine",
    )(parts, x, post, steer)


def cut_kernel(x_ref, o_ref):
    width = o_ref.shape[2]
    for t in range(o_ref.shape[0]):
        o_ref[t] = x_ref[:, pl.ds(t * width, width)]


def cut_call(x, lanes):
    rows, width = x.shape
    return pl.pallas_call(
        cut_kernel,
        out_shape=jax.ShapeDtypeStruct((lanes, rows, width // lanes), x.dtype),
        in_specs=[VMEM],
        out_specs=VMEM,
        compiler_params=pltpu.CompilerParams(vmem_limit_bytes=4 << 20),
        name="cut",
    )(x)


def merge_kernel(from_ref, p_ref, o_ref):
    per = p_ref.shape[1]
    for k in range(o_ref.shape[0] // per):
        o_ref[pl.ds(k * per, per), :] = p_ref[from_ref[0] + k]


def merge_call(source, pieces, rows):
    return pl.pallas_call(
        merge_kernel,
        out_shape=jax.ShapeDtypeStruct((rows, pieces.shape[2]), pieces.dtype),
        in_specs=[SMEM, VMEM],
        out_specs=VMEM,
        compiler_params=pltpu.CompilerParams(vmem_limit_bytes=4 << 20),
        name="merge",
    )(source, pieces)


def swap(value, axis):
    return lax.all_to_all(value, axis, 0, 0, tiled=True)


def on_device(
    resid, pre_gain, post_gain, w_query, w_key, w_value, w_out, key_cache, value_cache,
    lengths, concept, steer_layer, strength, directions,
):
    sections = lax.axis_size("section")
    lanes = lax.axis_size("tensor")
    section = lax.axis_index("section")
    lane = lax.axis_index("tensor")
    batch, width = resid.shape
    planes, core, plane = sections // 2, section % 2, section // 2
    rows = batch * planes
    per = rows // lanes
    start = core * rows

    def shifted(value, target):
        pairs = [(s * lanes + t, target(s) * lanes + t) for s in range(sections) for t in range(lanes)]
        return lax.ppermute(value, ("section", "tensor"), pairs)

    def other(value):
        return shifted(value, lambda s: s ^ 1)

    def mine(value):
        return lax.dynamic_slice_in_dim(value, start, rows, 0)

    here = (w_query[0], w_key[0], w_value[0], w_out[0],
            key_cache.reshape(batch * sections, *key_cache.shape[3:]),
            value_cache.reshape(batch * sections, *value_cache.shape[3:]))
    here = tuple(pltpu.with_memory_space_constraint(value, pltpu.HBM) for value in here)
    there = tuple(other(value) for value in here)
    lens = mine(lengths)
    half = HD // 2
    frequency = 10000.0 ** (-(jnp.arange(half, dtype=jnp.float32) * 2.0) / HD)
    angles = lens.astype(jnp.float32)[:, None] * frequency[None, :]
    cosine, sine = jnp.cos(angles), jnp.sin(angles)
    cos = jnp.concatenate([cosine, cosine], axis=1)
    sin = jnp.concatenate([-sine, sine], axis=1)
    lens = jnp.broadcast_to(lens[:, None], (rows, HD))

    everyone = swap(jnp.broadcast_to(resid[None], (sections, batch, width)), "section")
    pre, post = [
        [jnp.where(core == 0, own, far), jnp.where(core == 0, far, own)]
        for own, far in ((pre_gain, other(pre_gain)), (post_gain, other(post_gain)))
    ]
    ids = jnp.arange(directions.shape[0], dtype=jnp.int32)
    one_hot = (mine(concept)[:, None] == ids[None, :]).astype(jnp.bfloat16)
    picked = jnp.dot(one_hot, directions, preferred_element_type=jnp.float32).astype(jnp.bfloat16)
    state = mine(everyone.reshape(batch * sections, width))
    both = jnp.concatenate(
        [jnp.broadcast_to(state[None], (lanes, rows, width)), picked.reshape(lanes, per, width)], axis=1
    )
    both = swap(both, "tensor")
    x = lax.dynamic_slice_in_dim(both, lane * per, per, 1).transpose(1, 0, 2).reshape(per, D)
    vectors = both[:, rows:].transpose(1, 0, 2).reshape(per, D).astype(jnp.float32)
    row = start + lane * per
    strengths = lax.dynamic_slice_in_dim(strength, row, per, 0)
    layers = lax.dynamic_slice_in_dim(steer_layer, row, per, 0)
    steers = [
        (strengths * (layers == 2 * plane + k).astype(jnp.float32))[:, None] * vectors for k in range(2)
    ]

    sels = jnp.stack([core, (plane == 0).astype(jnp.int32)]).astype(jnp.int32)
    turns = [(plane == p).astype(jnp.int32).reshape(1) for p in range(planes)]
    cos, sin, lens, pre, post, steers, sels = lax.optimization_barrier(
        (cos, sin, lens, pre, post, steers, sels)
    )

    def gathered(x):
        return swap(jnp.broadcast_to(x[None], (lanes, per, D)), "tensor")

    share = batch // per
    source = section % planes * share
    source = source.astype(jnp.int32).reshape(1)
    x, both, source, turns = lax.optimization_barrier((x, both, source, turns))
    full = both
    for p in range(planes):
        if p:
            x = shifted(x, lambda s: (s + 2) % sections)
            full = gathered(x)
        if p:
            parts = layer_call(turns[p], full, per, pre[0], cos, sin, lens, loaded[0])
        else:
            parts, *loaded = opening_call(sels, full, per, pre[0], cos, sin, lens, here, there)
        x, copies = combine_call(swap(parts, "tensor"), x, post[0], steers[0], lanes)
        parts = layer_call(turns[p], swap(copies, "tensor"), per, pre[1], cos, sin, lens, loaded[1])
        x, = combine_call(swap(parts, "tensor"), x, post[1], steers[1], 0)
    pairs = [
        ((sections - 2 + c) * lanes + t, (c * planes + t // share) * lanes + t)
        for c in range(2)
        for t in range(lanes)
    ]
    x = lax.ppermute(x, ("section", "tensor"), pairs)
    return merge_call(source, swap(cut_call(x, lanes), "tensor"), batch)


def solution(mesh):
    placed = (
        P("section", "tensor"),
        P("section", None),
        P("section", None),
        P("section", None, "tensor"),
        P("section", None, "tensor"),
        P("section", None, "tensor"),
        P("section", "tensor", None),
        P("section", None, "tensor", None, None),
        P("section", None, "tensor", None, None),
        P(),
        P(),
        P(),
        P(),
        P(None, "tensor"),
    )
    return jax.shard_map(
        on_device, mesh=mesh, in_specs=placed, out_specs=P("section", "tensor"), check_vma=False
    )
```

```python
import jax
import jax.numpy as jnp
from jax import lax
from jax.experimental import pallas as pl
from jax.experimental.pallas import tpu as pltpu
from jax.sharding import PartitionSpec as P

D = 4608
HEADS = 32
KVH = 16
HD = 128
GROUP = HEADS // KVH
QW = GROUP * HD
CHUNKS = 6
DC = D // CHUNKS
EPS = 1e-06
CAP = 50.0
SCALE = float(D // HEADS) ** (-0.5)
SMEM = pl.BlockSpec(memory_space=pltpu.SMEM)
VMEM = pl.BlockSpec(memory_space=pltpu.VMEM)
ANY = pl.BlockSpec(memory_space=pl.ANY)


def turn(v, cos, sin):
    return v * cos + pltpu.roll(v, HD // 2, 1) * sin


def project(x_ref, pre_ref, cos_ref, sin_ref, len_ref, w, wo, kc, vc, o_ref, xs, ho, arrived):
    rows = xs.shape[0]
    ctx = kc.shape[1]
    blocks, per = o_ref.shape[0], o_ref.shape[1]
    if x_ref.shape[1] == per:
        for b in range(blocks):
            xs[pl.ds(b * per, per), :] = x_ref[b]
    else:
        width = x_ref.shape[2]
        for b in range(blocks):
            xs[:, pl.ds(b * width, width)] = x_ref[b, pl.ds(0, rows), :]
    acc = jnp.zeros((rows, QW + 2 * HD), jnp.float32)
    squares = jnp.zeros((rows, 1), jnp.float32)
    for c in range(CHUNKS):
        part = xs[:, pl.ds(c * DC, DC)].astype(jnp.float32)
        squares += jnp.sum(part * part, axis=1, keepdims=True)
        scaled = (part * pre_ref[:, pl.ds(c * DC, DC)]).astype(jnp.bfloat16)
        arrived(c)
        acc += jnp.dot(scaled, w[pl.ds(c * DC, DC), :], preferred_element_type=jnp.float32)
    acc = acc * lax.rsqrt(squares / D + EPS)
    cos, sin = cos_ref[...], sin_ref[...]
    heads = [turn(acc[:, h * HD:(h + 1) * HD], cos, sin).astype(jnp.bfloat16) for h in range(GROUP)]
    new_k = turn(acc[:, QW:QW + HD], cos, sin).astype(jnp.bfloat16).astype(jnp.float32)
    new_v = acc[:, QW + HD:].astype(jnp.bfloat16).astype(jnp.float32)
    arrived(CHUNKS)
    n = rows
    col = lax.broadcasted_iota(jnp.int32, (GROUP * n, n * ctx), 1)
    row = lax.broadcasted_iota(jnp.int32, (GROUP * n, n * ctx), 0)
    rel = col - (row % n) * ctx
    rel = jnp.where(rel < 0, n * ctx, rel)
    for g in range(rows // n):
        lo, hi = g * n, (g + 1) * n
        q = jnp.concatenate([h[lo:hi].astype(jnp.float32) for h in heads], axis=0)
        nk = jnp.concatenate([new_k[lo:hi]] * GROUP, axis=0)
        nv = jnp.concatenate([new_v[lo:hi]] * GROUP, axis=0)
        ln = jnp.concatenate([len_ref[lo:hi, :1]] * GROUP, axis=0)
        keys = kc[pl.ds(lo, n)].reshape(n * ctx, HD)
        vals = vc[pl.ds(lo, n)].reshape(n * ctx, HD)
        s = lax.dot_general(
            q.astype(jnp.bfloat16), keys, (((1,), (1,)), ((), ())), preferred_element_type=jnp.float32
        )
        own = jnp.sum(q * nk, axis=1, keepdims=True)
        wt = jnp.exp(CAP * jnp.tanh(s * (SCALE / CAP)) - CAP)
        wt = jnp.where(rel < ln, wt, 0.0)
        own_w = jnp.exp(CAP * jnp.tanh(own * (SCALE / CAP)) - CAP)
        total = jnp.sum(wt, axis=1, keepdims=True) + own_w
        probs = (wt / total).astype(jnp.bfloat16)
        own_p = (own_w / total).astype(jnp.bfloat16).astype(jnp.float32)
        mixed = jnp.dot(probs, vals, preferred_element_type=jnp.float32) + own_p * nv
        for h in range(GROUP):
            ho[pl.ds(lo, n), pl.ds(h * HD, HD)] = mixed[h * n:(h + 1) * n]
    arrived(CHUNKS + 1)
    lhs = ho[...].astype(jnp.bfloat16)
    for c in range(CHUNKS):
        at = pl.ds(c * DC, DC)
        out = jnp.dot(lhs, wo[:, at], preferred_element_type=jnp.float32).astype(jnp.bfloat16)
        for b in range(blocks):
            o_ref[b, :, at] = out[b * per:(b + 1) * per]


def layer_kernel(on_ref, x_ref, pre_ref, cos_ref, sin_ref, len_ref, w, wo, kc, vc, o_ref, xs, ho):
    @pl.when(on_ref[0] != 0)
    def _():
        project(x_ref, pre_ref, cos_ref, sin_ref, len_ref, w, wo, kc, vc, o_ref, xs, ho, lambda step: None)


def opening_kernel(
    sel_ref, x_ref, pre_ref, cos_ref, sin_ref, len_ref,
    wq_a, wk_a, wv_a, wo_a, kc_a, vc_a,
    wq_b, wk_b, wv_b, wo_b, kc_b, vc_b,
    o_ref, w0, wo0, kc0, vc0, w1, wo1, kc1, vc1,
    xs, ho, wsem, sem, late_sem,
):
    rows = xs.shape[0]
    mine = pl.ds(pl.multiple_of(sel_ref[0] * rows, rows), rows)
    here = (wq_a, wk_a, wv_a, wo_a, kc_a, vc_a)
    there = (wq_b, wk_b, wv_b, wo_b, kc_b, vc_b)

    def pieces(source, w, at):
        return (
            (source[0].at[at], w.at[at, pl.ds(0, QW)]),
            (source[1].at[at], w.at[at, pl.ds(QW, HD)]),
            (source[2].at[at], w.at[at, pl.ds(QW + HD, HD)]),
        )

    def early(source):
        steps = []
        for c in range(CHUNKS):
            at = pl.ds(c * DC, DC)
            steps.append([
                pltpu.make_async_copy(src, dst, wsem.at[3 * c + i])
                for i, (src, dst) in enumerate(pieces(source, w0, at))
            ])
        steps.append([
            pltpu.make_async_copy(source[4].at[mine], kc0, sem.at[0]),
            pltpu.make_async_copy(source[5].at[mine], vc0, sem.at[1]),
        ])
        steps.append([pltpu.make_async_copy(source[3], wo0, sem.at[2])])
        return steps

    def late(source):
        copies = [
            pltpu.make_async_copy(src, dst, late_sem.at[i])
            for i, (src, dst) in enumerate(pieces(source, w1, pl.ds(0, D)))
        ]
        return copies + [
            pltpu.make_async_copy(source[4].at[mine], kc1, late_sem.at[3]),
            pltpu.make_async_copy(source[5].at[mine], vc1, late_sem.at[4]),
            pltpu.make_async_copy(source[3], wo1, late_sem.at[5]),
        ]

    first, second = early(here), late(there)

    def begin_early(steps):
        for step in steps:
            for copy in step:
                copy.start()

    @pl.when(sel_ref[0] == 0)
    def _():
        begin_early(first)

    @pl.when(sel_ref[0] != 0)
    def _():
        begin_early(early(there))

    def begin_late():
        @pl.when(sel_ref[0] == 0)
        def _():
            for copy in second:
                copy.start()

        @pl.when(sel_ref[0] != 0)
        def _():
            for copy in late(here):
                copy.start()

    def arrived(step):
        for copy in first[step]:
            copy.wait()
        if step == CHUNKS - 1:
            begin_late()

    @pl.when(sel_ref[1] != 0)
    def _():
        project(x_ref, pre_ref, cos_ref, sin_ref, len_ref, w0, wo0, kc0, vc0, o_ref, xs, ho, arrived)

    @pl.when(sel_ref[1] == 0)
    def _():
        for step in range(len(first)):
            arrived(step)

    for copy in second:
        copy.wait()


def opening_call(sel, x, per, pre, cos, sin, lens, here, there):
    wo, kc, vc = here[3:]
    rows = lens.shape[0]
    kept = [(D, QW + 2 * HD), wo.shape, (rows,) + kc.shape[1:], (rows,) + vc.shape[1:]]
    shapes = [(rows // per, per, D)] + kept + kept
    out, *loaded = pl.pallas_call(
        opening_kernel,
        out_shape=[jax.ShapeDtypeStruct(shape, jnp.bfloat16) for shape in shapes],
        in_specs=[SMEM] + [VMEM] * 5 + [ANY] * 3 + [VMEM] + [ANY] * 8,
        out_specs=[VMEM] * 9,
        scratch_shapes=[
            pltpu.VMEM((rows, D), jnp.bfloat16),
            pltpu.VMEM((rows, QW), jnp.float32),
            pltpu.SemaphoreType.DMA((3 * CHUNKS,)),
            pltpu.SemaphoreType.DMA((3,)),
            pltpu.SemaphoreType.DMA((6,)),
        ],
        compiler_params=pltpu.CompilerParams(vmem_limit_bytes=28 << 20),
        name="opening",
    )(sel, x, pre, cos, sin, lens, *here, *there)
    return out, loaded[:4], loaded[4:]


def keep_kernel(wo_hbm, wo, sem):
    copy = pltpu.make_async_copy(wo_hbm, wo, sem)
    copy.start()
    copy.wait()


def keep_call(wo):
    return pl.pallas_call(
        keep_kernel,
        out_shape=pltpu.VMEM(wo.shape, wo.dtype),
        in_specs=[ANY],
        out_specs=VMEM,
        scratch_shapes=[pltpu.SemaphoreType.DMA],
        compiler_params=pltpu.CompilerParams(vmem_limit_bytes=4 << 20),
        cost_estimate=pl.CostEstimate(flops=0, bytes_accessed=4 * wo.size, transcendentals=0),
        name="keep",
    )(wo)


def layer_call(on, x, per, pre, cos, sin, lens, loaded):
    rows = lens.shape[0]
    return pl.pallas_call(
        layer_kernel,
        out_shape=jax.ShapeDtypeStruct((rows // per, per, D), jnp.bfloat16),
        in_specs=[SMEM] + [VMEM] * 9,
        out_specs=VMEM,
        scratch_shapes=[pltpu.VMEM((rows, D), jnp.bfloat16), pltpu.VMEM((rows, QW), jnp.float32)],
        compiler_params=pltpu.CompilerParams(vmem_limit_bytes=14 << 20),
        name="layer",
    )(on, x, pre, cos, sin, lens, *loaded)


def combine_kernel(p_ref, x_ref, post_ref, steer_ref, o_ref, *copies_ref):
    total = p_ref[0].astype(jnp.float32)
    for b in range(1, p_ref.shape[0]):
        total += p_ref[b].astype(jnp.float32)
    factor = lax.rsqrt(jnp.mean(total * total, axis=1, keepdims=True) + EPS)
    post = total * factor * post_ref[...]
    out = (x_ref[...].astype(jnp.float32) + post + steer_ref[...]).astype(jnp.bfloat16)
    o_ref[...] = out
    for ref in copies_ref:
        for b in range(ref.shape[0]):
            ref[b] = out


def combine_call(parts, x, post, steer, copies):
    shapes = [x.shape] + ([(copies,) + x.shape] if copies else [])
    return pl.pallas_call(
        combine_kernel,
        out_shape=[jax.ShapeDtypeStruct(shape, x.dtype) for shape in shapes],
        in_specs=[VMEM] * 4,
        out_specs=[VMEM] * len(shapes),
        compiler_params=pltpu.CompilerParams(vmem_limit_bytes=8 << 20),
        name="combine",
    )(parts, x, post, steer)


def cut_kernel(x_ref, o_ref):
    width = o_ref.shape[2]
    for t in range(o_ref.shape[0]):
        o_ref[t] = x_ref[:, pl.ds(t * width, width)]


def cut_call(x, lanes):
    rows, width = x.shape
    return pl.pallas_call(
        cut_kernel,
        out_shape=jax.ShapeDtypeStruct((lanes, rows, width // lanes), x.dtype),
        in_specs=[VMEM],
        out_specs=VMEM,
        compiler_params=pltpu.CompilerParams(vmem_limit_bytes=4 << 20),
        name="cut",
    )(x)


def merge_kernel(from_ref, p_ref, o_ref):
    per = p_ref.shape[1]
    for k in range(o_ref.shape[0] // per):
        o_ref[pl.ds(k * per, per), :] = p_ref[from_ref[0] + k]


def merge_call(source, pieces, rows):
    return pl.pallas_call(
        merge_kernel,
        out_shape=jax.ShapeDtypeStruct((rows, pieces.shape[2]), pieces.dtype),
        in_specs=[SMEM, VMEM],
        out_specs=VMEM,
        compiler_params=pltpu.CompilerParams(vmem_limit_bytes=4 << 20),
        name="merge",
    )(source, pieces)


def swap(value, axis):
    return lax.all_to_all(value, axis, 0, 0, tiled=True)


def on_device(
    resid, pre_gain, post_gain, w_query, w_key, w_value, w_out, key_cache, value_cache,
    lengths, concept, steer_layer, strength, directions,
):
    sections = lax.axis_size("section")
    lanes = lax.axis_size("tensor")
    section = lax.axis_index("section")
    lane = lax.axis_index("tensor")
    batch, width = resid.shape
    planes, core, plane = sections // 2, section % 2, section // 2
    rows = batch * planes
    per = rows // lanes
    start = core * rows

    def shifted(value, target):
        pairs = [(s * lanes + t, target(s) * lanes + t) for s in range(sections) for t in range(lanes)]
        return lax.ppermute(value, ("section", "tensor"), pairs)

    def other(value):
        return shifted(value, lambda s: s ^ 1)

    def mine(value):
        return lax.dynamic_slice_in_dim(value, start, rows, 0)

    here = (w_query[0], w_key[0], w_value[0], w_out[0],
            key_cache.reshape(batch * sections, *key_cache.shape[3:]),
            value_cache.reshape(batch * sections, *value_cache.shape[3:]))
    here = tuple(pltpu.with_memory_space_constraint(value, pltpu.HBM) for value in here)
    there = tuple(other(value) for value in here)
    lens = mine(lengths)
    half = HD // 2
    frequency = 10000.0 ** (-(jnp.arange(half, dtype=jnp.float32) * 2.0) / HD)
    angles = lens.astype(jnp.float32)[:, None] * frequency[None, :]
    cosine, sine = jnp.cos(angles), jnp.sin(angles)
    cos = jnp.concatenate([cosine, cosine], axis=1)
    sin = jnp.concatenate([-sine, sine], axis=1)
    lens = jnp.broadcast_to(lens[:, None], (rows, HD))

    everyone = swap(jnp.broadcast_to(resid[None], (sections, batch, width)), "section")
    pre, post = [
        [jnp.where(core == 0, own, far), jnp.where(core == 0, far, own)]
        for own, far in ((pre_gain, other(pre_gain)), (post_gain, other(post_gain)))
    ]
    ids = jnp.arange(directions.shape[0], dtype=jnp.int32)
    one_hot = (mine(concept)[:, None] == ids[None, :]).astype(jnp.bfloat16)
    picked = jnp.dot(one_hot, directions, preferred_element_type=jnp.float32).astype(jnp.bfloat16)
    state = mine(everyone.reshape(batch * sections, width))
    both = jnp.concatenate(
        [jnp.broadcast_to(state[None], (lanes, rows, width)), picked.reshape(lanes, per, width)], axis=1
    )
    both, out_weight = lax.optimization_barrier((both, here[3]))
    both = swap(both, "tensor")
    here = here[:3] + (keep_call(out_weight),) + here[4:]
    x = lax.dynamic_slice_in_dim(both, lane * per, per, 1).transpose(1, 0, 2).reshape(per, D)
    vectors = both[:, rows:].transpose(1, 0, 2).reshape(per, D).astype(jnp.float32)
    row = start + lane * per
    strengths = lax.dynamic_slice_in_dim(strength, row, per, 0)
    layers = lax.dynamic_slice_in_dim(steer_layer, row, per, 0)
    steers = [
        (strengths * (layers == 2 * plane + k).astype(jnp.float32))[:, None] * vectors for k in range(2)
    ]

    sels = jnp.stack([core, (plane == 0).astype(jnp.int32)]).astype(jnp.int32)
    turns = [(plane == p).astype(jnp.int32).reshape(1) for p in range(planes)]
    cos, sin, lens, pre, post, steers, sels = lax.optimization_barrier(
        (cos, sin, lens, pre, post, steers, sels)
    )

    def gathered(x):
        return swap(jnp.broadcast_to(x[None], (lanes, per, D)), "tensor")

    share = batch // per
    source = section % planes * share
    source = source.astype(jnp.int32).reshape(1)
    x, both, source, turns = lax.optimization_barrier((x, both, source, turns))
    full = both
    for p in range(planes):
        if p:
            x = shifted(x, lambda s: (s + 2) % sections)
            full = gathered(x)
        if p:
            parts = layer_call(turns[p], full, per, pre[0], cos, sin, lens, loaded[0])
        else:
            parts, *loaded = opening_call(sels, full, per, pre[0], cos, sin, lens, here, there)
        x, copies = combine_call(swap(parts, "tensor"), x, post[0], steers[0], lanes)
        parts = layer_call(turns[p], swap(copies, "tensor"), per, pre[1], cos, sin, lens, loaded[1])
        x, = combine_call(swap(parts, "tensor"), x, post[1], steers[1], 0)
    pairs = [
        ((sections - 2 + c) * lanes + t, (c * planes + t // share) * lanes + t)
        for c in range(2)
        for t in range(lanes)
    ]
    x = lax.ppermute(x, ("section", "tensor"), pairs)
    return merge_call(source, swap(cut_call(x, lanes), "tensor"), batch)


def solution(mesh):
    placed = (
        P("section", "tensor"),
        P("section", None),
        P("section", None),
        P("section", None, "tensor"),
        P("section", None, "tensor"),
        P("section", None, "tensor"),
        P("section", "tensor", None),
        P("section", None, "tensor", None, None),
        P("section", None, "tensor", None, None),
        P(),
        P(),
        P(),
        P(),
        P(None, "tensor"),
    )
    return jax.shard_map(
        on_device, mesh=mesh, in_specs=placed, out_specs=P("section", "tensor"), check_vma=False
    )
```

```python
import jax
import jax.numpy as jnp
from jax import lax
from jax.experimental import pallas as pl
from jax.experimental.pallas import tpu as pltpu
from jax.sharding import PartitionSpec as P

D = 4608
HEADS = 32
KVH = 16
HD = 128
GROUP = HEADS // KVH
QW = GROUP * HD
CHUNKS = 6
DC = D // CHUNKS
EPS = 1e-06
CAP = 50.0
SCALE = float(D // HEADS) ** (-0.5)
SMEM = pl.BlockSpec(memory_space=pltpu.SMEM)
VMEM = pl.BlockSpec(memory_space=pltpu.VMEM)
ANY = pl.BlockSpec(memory_space=pl.ANY)


def turn(v, cos, sin):
    return v * cos + pltpu.roll(v, HD // 2, 1) * sin


def project(x_ref, pre_ref, cos_ref, sin_ref, len_ref, w, wo, kc, vc, o_ref, xs, ho, arrived):
    rows = xs.shape[0]
    ctx = kc.shape[1]
    blocks, per = o_ref.shape[0], o_ref.shape[1]
    if x_ref.shape[1] == per:
        for b in range(blocks):
            xs[pl.ds(b * per, per), :] = x_ref[b]
    else:
        width = x_ref.shape[2]
        for b in range(blocks):
            xs[:, pl.ds(b * width, width)] = x_ref[b, pl.ds(0, rows), :]
    acc = jnp.zeros((rows, QW + 2 * HD), jnp.float32)
    squares = jnp.zeros((rows, 1), jnp.float32)
    for c in range(CHUNKS):
        part = xs[:, pl.ds(c * DC, DC)].astype(jnp.float32)
        squares += jnp.sum(part * part, axis=1, keepdims=True)
        scaled = (part * pre_ref[:, pl.ds(c * DC, DC)]).astype(jnp.bfloat16)
        arrived(c)
        acc += jnp.dot(scaled, w[pl.ds(c * DC, DC), :], preferred_element_type=jnp.float32)
    acc = acc * lax.rsqrt(squares / D + EPS)
    cos, sin = cos_ref[...], sin_ref[...]
    heads = [turn(acc[:, h * HD:(h + 1) * HD], cos, sin).astype(jnp.bfloat16) for h in range(GROUP)]
    new_k = turn(acc[:, QW:QW + HD], cos, sin).astype(jnp.bfloat16).astype(jnp.float32)
    new_v = acc[:, QW + HD:].astype(jnp.bfloat16).astype(jnp.float32)
    arrived(CHUNKS)
    n = rows
    col = lax.broadcasted_iota(jnp.int32, (GROUP * n, n * ctx), 1)
    row = lax.broadcasted_iota(jnp.int32, (GROUP * n, n * ctx), 0)
    rel = col - (row % n) * ctx
    rel = jnp.where(rel < 0, n * ctx, rel)
    for g in range(rows // n):
        lo, hi = g * n, (g + 1) * n
        q = jnp.concatenate([h[lo:hi].astype(jnp.float32) for h in heads], axis=0)
        nk = jnp.concatenate([new_k[lo:hi]] * GROUP, axis=0)
        nv = jnp.concatenate([new_v[lo:hi]] * GROUP, axis=0)
        ln = jnp.concatenate([len_ref[lo:hi, :1]] * GROUP, axis=0)
        keys = kc[pl.ds(lo, n)].reshape(n * ctx, HD)
        vals = vc[pl.ds(lo, n)].reshape(n * ctx, HD)
        s = lax.dot_general(
            q.astype(jnp.bfloat16), keys, (((1,), (1,)), ((), ())), preferred_element_type=jnp.float32
        )
        own = jnp.sum(q * nk, axis=1, keepdims=True)
        wt = jnp.exp(CAP * jnp.tanh(s * (SCALE / CAP)) - CAP)
        wt = jnp.where(rel < ln, wt, 0.0)
        own_w = jnp.exp(CAP * jnp.tanh(own * (SCALE / CAP)) - CAP)
        total = jnp.sum(wt, axis=1, keepdims=True) + own_w
        probs = (wt / total).astype(jnp.bfloat16)
        own_p = (own_w / total).astype(jnp.bfloat16).astype(jnp.float32)
        mixed = jnp.dot(probs, vals, preferred_element_type=jnp.float32) + own_p * nv
        for h in range(GROUP):
            ho[pl.ds(lo, n), pl.ds(h * HD, HD)] = mixed[h * n:(h + 1) * n]
    arrived(CHUNKS + 1)
    lhs = ho[...].astype(jnp.bfloat16)
    for c in range(CHUNKS):
        at = pl.ds(c * DC, DC)
        out = jnp.dot(lhs, wo[:, at], preferred_element_type=jnp.float32).astype(jnp.bfloat16)
        for b in range(blocks):
            o_ref[b, :, at] = out[b * per:(b + 1) * per]


def layer_kernel(on_ref, x_ref, pre_ref, cos_ref, sin_ref, len_ref, w, wo, kc, vc, o_ref, xs, ho):
    @pl.when(on_ref[0] != 0)
    def _():
        project(x_ref, pre_ref, cos_ref, sin_ref, len_ref, w, wo, kc, vc, o_ref, xs, ho, lambda step: None)


def opening_kernel(
    sel_ref, x_ref, pre_ref, cos_ref, sin_ref, len_ref,
    wq_a, wk_a, wv_a, wo_a, kc_a, vc_a,
    wq_b, wk_b, wv_b, wo_b, kc_b, vc_b,
    o_ref, w0, wo0, kc0, vc0, w1, wo1, kc1, vc1,
    xs, ho, wsem, sem, late_sem,
):
    rows = xs.shape[0]
    mine = pl.ds(pl.multiple_of(sel_ref[0] * rows, rows), rows)
    here = (wq_a, wk_a, wv_a, wo_a, kc_a, vc_a)
    there = (wq_b, wk_b, wv_b, wo_b, kc_b, vc_b)

    def pieces(source, w, at):
        return (
            (source[0].at[at], w.at[at, pl.ds(0, QW)]),
            (source[1].at[at], w.at[at, pl.ds(QW, HD)]),
            (source[2].at[at], w.at[at, pl.ds(QW + HD, HD)]),
        )

    def early(source):
        steps = []
        for c in range(CHUNKS):
            at = pl.ds(c * DC, DC)
            steps.append([
                pltpu.make_async_copy(src, dst, wsem.at[3 * c + i])
                for i, (src, dst) in enumerate(pieces(source, w0, at))
            ])
        steps.append([
            pltpu.make_async_copy(source[4].at[mine], kc0, sem.at[0]),
            pltpu.make_async_copy(source[5].at[mine], vc0, sem.at[1]),
        ])
        steps.append([pltpu.make_async_copy(source[3], wo0, sem.at[2])])
        return steps

    def late(source):
        copies = [
            pltpu.make_async_copy(src, dst, late_sem.at[i])
            for i, (src, dst) in enumerate(pieces(source, w1, pl.ds(0, D)))
        ]
        return copies + [
            pltpu.make_async_copy(source[4].at[mine], kc1, late_sem.at[3]),
            pltpu.make_async_copy(source[5].at[mine], vc1, late_sem.at[4]),
            pltpu.make_async_copy(source[3], wo1, late_sem.at[5]),
        ]

    first, second = early(here), late(there)

    def begin_early(steps):
        for step in steps:
            for copy in step:
                copy.start()

    @pl.when(sel_ref[0] == 0)
    def _():
        begin_early(first)

    @pl.when(sel_ref[0] != 0)
    def _():
        begin_early(early(there))

    def begin_late():
        @pl.when(sel_ref[0] == 0)
        def _():
            for copy in second:
                copy.start()

        @pl.when(sel_ref[0] != 0)
        def _():
            for copy in late(here):
                copy.start()

    def arrived(step):
        for copy in first[step]:
            copy.wait()
        if step == CHUNKS - 3:
            begin_late()

    @pl.when(sel_ref[1] != 0)
    def _():
        project(x_ref, pre_ref, cos_ref, sin_ref, len_ref, w0, wo0, kc0, vc0, o_ref, xs, ho, arrived)

    @pl.when(sel_ref[1] == 0)
    def _():
        for step in range(len(first)):
            arrived(step)

    for copy in second:
        copy.wait()


def opening_call(sel, x, per, pre, cos, sin, lens, here, there):
    wo, kc, vc = here[3:]
    rows = lens.shape[0]
    kept = [(D, QW + 2 * HD), wo.shape, (rows,) + kc.shape[1:], (rows,) + vc.shape[1:]]
    shapes = [(rows // per, per, D)] + kept + kept
    out, *loaded = pl.pallas_call(
        opening_kernel,
        out_shape=[jax.ShapeDtypeStruct(shape, jnp.bfloat16) for shape in shapes],
        in_specs=[SMEM] + [VMEM] * 5 + [ANY] * 3 + [VMEM] + [ANY] * 8,
        out_specs=[VMEM] * 9,
        scratch_shapes=[
            pltpu.VMEM((rows, D), jnp.bfloat16),
            pltpu.VMEM((rows, QW), jnp.float32),
            pltpu.SemaphoreType.DMA((3 * CHUNKS,)),
            pltpu.SemaphoreType.DMA((3,)),
            pltpu.SemaphoreType.DMA((6,)),
        ],
        compiler_params=pltpu.CompilerParams(vmem_limit_bytes=28 << 20),
        name="opening",
    )(sel, x, pre, cos, sin, lens, *here, *there)
    return out, loaded[:4], loaded[4:]


def keep_kernel(wo_hbm, wo, sem):
    copy = pltpu.make_async_copy(wo_hbm, wo, sem)
    copy.start()
    copy.wait()


def keep_call(wo):
    return pl.pallas_call(
        keep_kernel,
        out_shape=pltpu.VMEM(wo.shape, wo.dtype),
        in_specs=[ANY],
        out_specs=VMEM,
        scratch_shapes=[pltpu.SemaphoreType.DMA],
        compiler_params=pltpu.CompilerParams(vmem_limit_bytes=4 << 20),
        cost_estimate=pl.CostEstimate(flops=0, bytes_accessed=4 * wo.size, transcendentals=0),
        name="keep",
    )(wo)


def layer_call(on, x, per, pre, cos, sin, lens, loaded):
    rows = lens.shape[0]
    return pl.pallas_call(
        layer_kernel,
        out_shape=jax.ShapeDtypeStruct((rows // per, per, D), jnp.bfloat16),
        in_specs=[SMEM] + [VMEM] * 9,
        out_specs=VMEM,
        scratch_shapes=[pltpu.VMEM((rows, D), jnp.bfloat16), pltpu.VMEM((rows, QW), jnp.float32)],
        compiler_params=pltpu.CompilerParams(vmem_limit_bytes=14 << 20),
        name="layer",
    )(on, x, pre, cos, sin, lens, *loaded)


def combine_kernel(p_ref, x_ref, post_ref, steer_ref, o_ref, *copies_ref):
    total = p_ref[0].astype(jnp.float32)
    for b in range(1, p_ref.shape[0]):
        total += p_ref[b].astype(jnp.float32)
    factor = lax.rsqrt(jnp.mean(total * total, axis=1, keepdims=True) + EPS)
    post = total * factor * post_ref[...]
    out = (x_ref[...].astype(jnp.float32) + post + steer_ref[...]).astype(jnp.bfloat16)
    o_ref[...] = out
    for ref in copies_ref:
        for b in range(ref.shape[0]):
            ref[b] = out


def combine_call(parts, x, post, steer, copies):
    shapes = [x.shape] + ([(copies,) + x.shape] if copies else [])
    return pl.pallas_call(
        combine_kernel,
        out_shape=[jax.ShapeDtypeStruct(shape, x.dtype) for shape in shapes],
        in_specs=[VMEM] * 4,
        out_specs=[VMEM] * len(shapes),
        compiler_params=pltpu.CompilerParams(vmem_limit_bytes=8 << 20),
        name="combine",
    )(parts, x, post, steer)


def cut_kernel(x_ref, o_ref):
    width = o_ref.shape[2]
    for t in range(o_ref.shape[0]):
        o_ref[t] = x_ref[:, pl.ds(t * width, width)]


def cut_call(x, lanes):
    rows, width = x.shape
    return pl.pallas_call(
        cut_kernel,
        out_shape=jax.ShapeDtypeStruct((lanes, rows, width // lanes), x.dtype),
        in_specs=[VMEM],
        out_specs=VMEM,
        compiler_params=pltpu.CompilerParams(vmem_limit_bytes=4 << 20),
        name="cut",
    )(x)


def merge_kernel(from_ref, p_ref, o_ref):
    per = p_ref.shape[1]
    for k in range(o_ref.shape[0] // per):
        o_ref[pl.ds(k * per, per), :] = p_ref[from_ref[0] + k]


def merge_call(source, pieces, rows):
    return pl.pallas_call(
        merge_kernel,
        out_shape=jax.ShapeDtypeStruct((rows, pieces.shape[2]), pieces.dtype),
        in_specs=[SMEM, VMEM],
        out_specs=VMEM,
        compiler_params=pltpu.CompilerParams(vmem_limit_bytes=4 << 20),
        name="merge",
    )(source, pieces)


def swap(value, axis):
    return lax.all_to_all(value, axis, 0, 0, tiled=True)


def on_device(
    resid, pre_gain, post_gain, w_query, w_key, w_value, w_out, key_cache, value_cache,
    lengths, concept, steer_layer, strength, directions,
):
    sections = lax.axis_size("section")
    lanes = lax.axis_size("tensor")
    section = lax.axis_index("section")
    lane = lax.axis_index("tensor")
    batch, width = resid.shape
    planes, core, plane = sections // 2, section % 2, section // 2
    rows = batch * planes
    per = rows // lanes
    start = core * rows

    def shifted(value, target):
        pairs = [(s * lanes + t, target(s) * lanes + t) for s in range(sections) for t in range(lanes)]
        return lax.ppermute(value, ("section", "tensor"), pairs)

    def other(value):
        return shifted(value, lambda s: s ^ 1)

    def mine(value):
        return lax.dynamic_slice_in_dim(value, start, rows, 0)

    here = (w_query[0], w_key[0], w_value[0], w_out[0],
            key_cache.reshape(batch * sections, *key_cache.shape[3:]),
            value_cache.reshape(batch * sections, *value_cache.shape[3:]))
    here = tuple(pltpu.with_memory_space_constraint(value, pltpu.HBM) for value in here)
    there = tuple(other(value) for value in here)
    lens = mine(lengths)
    half = HD // 2
    frequency = 10000.0 ** (-(jnp.arange(half, dtype=jnp.float32) * 2.0) / HD)
    angles = lens.astype(jnp.float32)[:, None] * frequency[None, :]
    cosine, sine = jnp.cos(angles), jnp.sin(angles)
    cos = jnp.concatenate([cosine, cosine], axis=1)
    sin = jnp.concatenate([-sine, sine], axis=1)
    lens = jnp.broadcast_to(lens[:, None], (rows, HD))

    everyone = swap(jnp.broadcast_to(resid[None], (sections, batch, width)), "section")
    pre, post = [
        [jnp.where(core == 0, own, far), jnp.where(core == 0, far, own)]
        for own, far in ((pre_gain, other(pre_gain)), (post_gain, other(post_gain)))
    ]
    ids = jnp.arange(directions.shape[0], dtype=jnp.int32)
    one_hot = (mine(concept)[:, None] == ids[None, :]).astype(jnp.bfloat16)
    picked = jnp.dot(one_hot, directions, preferred_element_type=jnp.float32).astype(jnp.bfloat16)
    state = mine(everyone.reshape(batch * sections, width))
    both = jnp.concatenate(
        [jnp.broadcast_to(state[None], (lanes, rows, width)), picked.reshape(lanes, per, width)], axis=1
    )
    both, out_weight = lax.optimization_barrier((both, here[3]))
    both = swap(both, "tensor")
    here = here[:3] + (keep_call(out_weight),) + here[4:]
    x = lax.dynamic_slice_in_dim(both, lane * per, per, 1).transpose(1, 0, 2).reshape(per, D)
    vectors = both[:, rows:].transpose(1, 0, 2).reshape(per, D).astype(jnp.float32)
    row = start + lane * per
    strengths = lax.dynamic_slice_in_dim(strength, row, per, 0)
    layers = lax.dynamic_slice_in_dim(steer_layer, row, per, 0)
    steers = [
        (strengths * (layers == 2 * plane + k).astype(jnp.float32))[:, None] * vectors for k in range(2)
    ]

    sels = jnp.stack([core, (plane == 0).astype(jnp.int32)]).astype(jnp.int32)
    turns = [(plane == p).astype(jnp.int32).reshape(1) for p in range(planes)]
    cos, sin, lens, pre, post, steers, sels = lax.optimization_barrier(
        (cos, sin, lens, pre, post, steers, sels)
    )

    def gathered(x):
        return swap(jnp.broadcast_to(x[None], (lanes, per, D)), "tensor")

    share = batch // per
    source = section % planes * share
    source = source.astype(jnp.int32).reshape(1)
    x, both, source, turns = lax.optimization_barrier((x, both, source, turns))
    full = both
    for p in range(planes):
        if p:
            x = shifted(x, lambda s: (s + 2) % sections)
            full = gathered(x)
        if p:
            parts = layer_call(turns[p], full, per, pre[0], cos, sin, lens, loaded[0])
        else:
            parts, *loaded = opening_call(sels, full, per, pre[0], cos, sin, lens, here, there)
        x, copies = combine_call(swap(parts, "tensor"), x, post[0], steers[0], lanes)
        parts = layer_call(turns[p], swap(copies, "tensor"), per, pre[1], cos, sin, lens, loaded[1])
        x, = combine_call(swap(parts, "tensor"), x, post[1], steers[1], 0)
    pairs = [
        ((sections - 2 + c) * lanes + t, (c * planes + t // share) * lanes + t)
        for c in range(2)
        for t in range(lanes)
    ]
    x = lax.ppermute(x, ("section", "tensor"), pairs)
    return merge_call(source, swap(cut_call(x, lanes), "tensor"), batch)


def solution(mesh):
    placed = (
        P("section", "tensor"),
        P("section", None),
        P("section", None),
        P("section", None, "tensor"),
        P("section", None, "tensor"),
        P("section", None, "tensor"),
        P("section", "tensor", None),
        P("section", None, "tensor", None, None),
        P("section", None, "tensor", None, None),
        P(),
        P(),
        P(),
        P(),
        P(None, "tensor"),
    )
    return jax.shard_map(
        on_device, mesh=mesh, in_specs=placed, out_specs=P("section", "tensor"), check_vma=False
    )
```
